32 devices in a mesh: chan: 2 (over x), bl: 16 (over z, y, core).
Axes of the slice: x: 2, y: 2, z: 4, core: 2. Of those that a mesh axis runs over, the one named last changes fastest.
Arguments:
- vis: bfloat16 [2, 8, 8192, 256], P(None, 'chan', 'bl'), may hold values from -6 to 6
- station_pair_index: int32 [8192, 2], P('bl'), may hold values from 0 to 511
- station_coords: float32 [512, 2], replicated, may hold values from -1 to 1
- dir_lm: float32 [60, 2], replicated, may hold values from -0.5 to 0.5
- time_beam: float32 [60, 256], replicated, may hold values from -6 to 6
- dir_cluster: int32 [60], replicated, may hold values from 0 to 11, as said below
- seed_block: int32 [64, 256, 8], P('bl'), may hold values from -8 to 8
Outputs:
- clean: bfloat16 [2, 8, 8192, 256], P(None, 'chan', 'bl')
- gains: float32 [64, 12], P('bl')
- consensus: float32 [12], replicated
The draws below stay inside these ranges and needn't reach their ends.
Inputs may be any that keep to these rules, and one draw needn't show every extreme that they name: `dir_cluster`: every cluster is named by some direction.
All inputs are finite; a program needn't handle non-finite values.
Results may differ from the reference program's by a relative error of at most 0.0029.
The reference program's roundings to bfloat16 on the way (of `response` and `basis`) count: a program that leaves them out, or rounds other values in their place, can miss the bound.
Values sent between devices are 32-bit elements; how exact they have to be, the bound alone decides.
A program may use at most 64 MiB of HBM per device.

```python
import jax
import jax.numpy as jnp
from jax import lax

TIME_SAMPLES = 256
DIRS = 60
STATION_COUNT = 512
RANK = 8
CL = 12
TILE = 128
SUB_ITERS = 3
ADMM_ITERS = 6
CHANNEL_COUNT = 8
BASELINE_COUNT = 8192
TILES = 64


def draw_dir_cluster(key, part):
    first_key, second_key, third_key = jax.random.split(key, 3)
    base = jax.random.permutation(first_key, CL).astype(jnp.int32)
    others = jax.random.randint(second_key, (DIRS - CL,), 0, CL).astype(jnp.int32)
    joined = jnp.concatenate([base, others])
    return jax.random.permutation(third_key, joined).astype(jnp.int32)


def set_ends(values, stream_key, low, high):
    place = [jax.random.randint(jax.random.fold_in(stream_key, axis), (), 0, length) for axis, length in enumerate(values.shape)]
    longest = values.shape.index(max(values.shape))
    next_to = place[:longest] + [(place[longest] + 1) % values.shape[longest]] + place[longest + 1:]
    return values.at[tuple(place)].set(low).at[tuple(next_to)].set(high)


def shard_levels(key, extent, shards, low, high):
    level = 1.0
    for position, blocks in shards:
        draws = jax.random.uniform(jax.random.fold_in(jax.random.fold_in(key, 6), position), (blocks,), jnp.float32, low / len(shards), high / len(shards))
        level = level * jnp.repeat(jnp.exp(draws), extent[position] // blocks).reshape((-1,) + (1,) * (len(extent) - 1 - position))
    return level


def noise(own_key, shape, scale, reach, pieces=(), kind=jnp.bfloat16):
    array = scale * jax.random.normal(own_key, shape, jnp.float32)
    if pieces:
        array = array * shard_levels(own_key, shape, pieces, -0.22, 0.18)
    return jnp.clip(array, -reach, reach).astype(kind)


def setup_inputs(seed: int = 0) -> dict:
    splits = jax.random.split(jax.random.key(seed), 8)
    vis = noise(splits[0], (2, CHANNEL_COUNT, BASELINE_COUNT, TIME_SAMPLES), 1.0, 6.0, ((1, 2), (2, 16)))
    station_pair_index = set_ends(jax.random.randint(splits[1], (BASELINE_COUNT, 2), 0, STATION_COUNT), jax.random.fold_in(splits[1], 1), 0, STATION_COUNT - 1).astype(jnp.int32)
    station_coords = jnp.clip(jax.random.uniform(splits[2], (STATION_COUNT, 2), jnp.float32, -1.0, 1.0), -1.0, 1.0)
    dir_lm = jnp.clip(jax.random.uniform(splits[3], (DIRS, 2), jnp.float32, -0.5, 0.5), -0.5, 0.5)
    time_beam = noise(splits[4], (DIRS, TIME_SAMPLES), 1.0, 6.0, (), jnp.float32)
    dir_cluster = draw_dir_cluster(jax.random.fold_in(splits[7], 71), 0)
    seed_block = set_ends(jax.random.randint(splits[6], (TILES, TIME_SAMPLES, RANK), -8, 9), jax.random.fold_in(splits[6], 1), -8, 8).astype(jnp.int32)
    return dict(vis=vis, station_pair_index=station_pair_index, station_coords=station_coords, dir_lm=dir_lm, time_beam=time_beam, dir_cluster=dir_cluster, seed_block=seed_block)


HIGHEST = lax.Precision.HIGHEST
PHASE_SCALE = 20.0
RHO_SCALE = 0.5

def orthonormal(block):
    square = jnp.dot(block.T, block, precision=HIGHEST)
    lower = jnp.linalg.cholesky(square)
    solved = jax.scipy.linalg.solve_triangular(lower, block.T, lower=True)
    return solved.T

def beam_fit(beam_proj, basis, time_beam):
    coeffs = jnp.dot(beam_proj, basis, precision=HIGHEST)
    inner = beam_proj - jnp.dot(coeffs, basis.T, precision=HIGHEST)
    return lax.optimization_barrier(jnp.sum(inner * time_beam, axis=-1))

def reference(vis, station_pair_index, station_coords, dir_lm, time_beam, dir_cluster, seed_block):
    uv = station_coords[station_pair_index[:, 0]] - station_coords[station_pair_index[:, 1]]
    geo = jnp.dot(dir_lm, uv.T, precision=HIGHEST)
    chan = jnp.arange(CHANNEL_COUNT).astype(jnp.float32)
    freq = 1.0 + chan / CHANNEL_COUNT
    phase = (PHASE_SCALE * freq)[None, :, None] * geo[:, None, :]
    response = jnp.stack([jnp.cos(phase), jnp.sin(phase)], axis=1).astype(jnp.bfloat16)

    def tile_work(index):
        start = (index * TILE).astype(jnp.int32)
        vis_tile = lax.dynamic_slice_in_dim(vis, start, TILE, 2).astype(jnp.float32)
        resp_tile = lax.dynamic_slice_in_dim(response, start, TILE, 3).astype(jnp.float32)
        gram = jnp.einsum('pcbt,pcbs->ts', vis_tile, vis_tile, precision=HIGHEST)
        beam_proj = jnp.einsum('dpcb,pcbt->dt', resp_tile, vis_tile, precision=HIGHEST)
        model_gram = jnp.einsum('dpcb,epcb->de', resp_tile, resp_tile, precision=HIGHEST)
        block = lax.dynamic_index_in_dim(seed_block, index, 0, keepdims=False).astype(jnp.float32)
        for step in range(SUB_ITERS):
            block = orthonormal(jnp.dot(gram, block, precision=HIGHEST))
        basis = block.astype(jnp.bfloat16).astype(jnp.float32)
        proj = jnp.einsum('pcbt,tk->pcbk', vis_tile, basis, precision=HIGHEST)
        correction = jnp.einsum('pcbk,tk->pcbt', proj, basis, precision=HIGHEST)
        filtered_visibility = (vis_tile - correction).astype(jnp.bfloat16)
        rhs_dir = beam_fit(beam_proj, basis, time_beam)
        return (filtered_visibility, rhs_dir, model_gram)
    filtered_visibility, rhs_dir, model_gram = lax.map(tile_work, jnp.arange(TILES).astype(jnp.int32))
    clean = jnp.transpose(filtered_visibility, (1, 2, 0, 3, 4)).reshape(2, CHANNEL_COUNT, BASELINE_COUNT, TIME_SAMPLES)
    beam_gram = jnp.dot(time_beam, time_beam.T, precision=HIGHEST)
    member = (dir_cluster[:, None] == jnp.arange(CL)[None, :]).astype(jnp.float32)
    weighted = model_gram * beam_gram[None]
    normal_matrix = jnp.einsum('dk,jde->jke', member, weighted, precision=HIGHEST)
    normal_matrix = jnp.einsum('jke,el->jkl', normal_matrix, member, precision=HIGHEST)
    rhs = jnp.einsum('dk,jd->jk', member, rhs_dir, precision=HIGHEST)
    rho = RHO_SCALE * jnp.trace(normal_matrix, axis1=1, axis2=2) / CL
    system = normal_matrix + rho[:, None, None] * jnp.eye(CL, dtype=jnp.float32)[None]
    lower = jnp.linalg.cholesky(system)
    center = jnp.zeros((CL,), jnp.float32)
    dual = jnp.zeros((TILES, CL), jnp.float32)
    solved = jnp.zeros((TILES, CL), jnp.float32)
    for step in range(ADMM_ITERS):
        target = rhs + rho[:, None] * (center[None, :] - dual)
        solved = jax.scipy.linalg.cho_solve((lower, True), target[..., None])[..., 0]
        center = lax.optimization_barrier(jnp.sum(solved + dual, axis=0)) / TILES
        dual = dual + solved - center[None, :]
    factor = jnp.sqrt(jnp.float32(CHANNEL_COUNT * TILE * TIME_SAMPLES))
    return (clean, solved * factor, center * factor)
```

```python
import functools

import jax
import jax.numpy as jnp
from jax import lax
from jax.experimental import pallas as pl
from jax.experimental.pallas import tpu as pltpu
from jax.sharding import PartitionSpec as P

CL = 12
SUB_ITERS = 3
ADMM_ITERS = 6
PHASE_SCALE = 20.0
RHO_SCALE = 0.5

HIGHEST = lax.Precision.HIGHEST
MESH = pl.DeviceIdType.MESH
F32 = jnp.float32
BF16 = jnp.bfloat16
LANES = 128
GROUP = 16
NT = (((1,), (1,)), ((), ()))
TN = (((0,), (0,)), ((), ()))


def split3(x):
    a = x.astype(BF16).astype(F32)
    rest = x - a
    b = rest.astype(BF16).astype(F32)
    return a, b, rest - b


def sincos(phase):
    k = jnp.floor(phase * F32(0.6366197723675814) + F32(0.5))
    r = phase - k * F32(1.5703125)
    r = r - k * F32(4.837512969970703125e-4)
    r = r - k * F32(7.54978995489188216e-8)
    r2 = r * r
    s = r + r * r2 * (F32(-1.6666654611e-1) + r2 * (F32(8.3321608736e-3) + r2 * F32(-1.9515295891e-4)))
    c = (F32(1.0) - F32(0.5) * r2) + r2 * r2 * (
        F32(4.166664568298827e-2) + r2 * (F32(-1.388731625493765e-3) + r2 * F32(2.443315711809948e-5))
    )
    ki = k.astype(jnp.int32)
    odd = (ki & 1) == 1
    cos = jnp.where(odd, s, c)
    sin = jnp.where(odd, c, s)
    cos = jnp.where(((ki + 1) & 2) == 2, -cos, cos)
    sin = jnp.where((ki & 2) == 2, -sin, sin)
    return cos, sin


def orthonormal(rows):
    sub = lax.broadcasted_iota(jnp.int32, (1, rows.shape[1], 1), 1)
    for k in range(rows.shape[1]):
        lead = rows[:, k : k + 1, :]
        dots = jnp.sum(rows * lead, axis=-1, keepdims=True)
        if k + 1 < rows.shape[1]:
            coef = jnp.where(sub > k, dots / dots[:, k : k + 1, :], F32(0.0))
            rows = rows - coef * lead
    norm = jnp.sum(rows * rows, axis=-1, keepdims=True)
    return rows / jnp.sqrt(norm)


def main_kernel(
    n_chan, n_bl, channels,
    vis_ref, pair_ref, coords_ref, lm_ref, tb_ref, cluster_ref, seed_ref,
    basis_ref, gains_ref, cons_ref,
    gsplit, resp, lmp, tbp, clp, coord_rows, uv_ref, beam, bsplit,
    ybuf, nbuf, mbuf, vbuf, send_sems, recv_sems,
):
    chan_dev, base_dev, times = vis_ref.shape[1:]
    tiles, rank = seed_ref.shape[0], seed_ref.shape[1]
    tile = base_dev // tiles
    dirs = lm_ref.shape[0]
    dpad = lmp.shape[0]
    stations = coords_ref.shape[1]
    n_all = n_chan * n_bl
    tiles_all = tiles * n_bl
    my_chan = lax.axis_index("chan")
    my_bl = lax.axis_index("bl")
    my_id = my_chan * n_bl + my_bl

    def everyone(off):
        other = lax.rem(my_id + off, n_all)
        return (lax.div(other, n_bl), lax.rem(other, n_bl))

    def along_chan(off):
        return (lax.rem(my_chan + off, n_chan), my_bl)

    def along_bl(off):
        return (my_chan, lax.rem(my_bl + off, n_bl))

    barrier = pltpu.get_barrier_semaphore()

    @pl.loop(1, n_all)
    def _(off):
        pl.semaphore_signal(barrier, inc=1, device_id=everyone(off), device_id_type=MESH)

    def push(buf, me, n, peer, phase):
        @pl.loop(1, n)
        def _(off):
            pltpu.make_async_remote_copy(
                src_ref=buf.at[me],
                dst_ref=buf.at[me],
                send_sem=send_sems.at[phase],
                recv_sem=recv_sems.at[phase],
                device_id=peer(off),
                device_id_type=MESH,
            ).start()

    def arrived(buf, n, phase):
        part = buf.at[pl.ds(0, n - 1)]
        pltpu.make_async_copy(part, part, recv_sems.at[phase]).wait()

    def sent(buf, n, phase):
        part = buf.at[pl.ds(0, n - 1)]
        pltpu.make_async_copy(part, part, send_sems.at[phase]).wait()

    def total(buf, n):
        out = buf[0]
        for i in range(1, n):
            out = out + buf[i]
        return out

    def vis_tile(j):
        return vis_ref[:, :, j * tile : (j + 1) * tile, :].reshape(2 * chan_dev * tile, times)

    first = []
    for j in range(tiles):
        v = vis_tile(j)
        gram = lax.dot_general(v, v, TN, preferred_element_type=F32)
        g1, g2, g3 = split3(gram)
        gsplit[j, 0] = g1.astype(BF16)
        gsplit[j, 1] = g2.astype(BF16)
        gsplit[j, 2] = g3.astype(BF16)
        seed = seed_ref[j].astype(F32)
        lhs = jnp.concatenate([seed, jnp.zeros_like(seed)], axis=0).astype(BF16)
        acc = jnp.dot(lhs, gsplit[j, 2], preferred_element_type=F32)
        acc = acc + jnp.dot(lhs, gsplit[j, 1], preferred_element_type=F32)
        acc = acc + jnp.dot(lhs, gsplit[j, 0], preferred_element_type=F32)
        first.append(acc[:rank])
    ybuf[0, my_chan] = jnp.concatenate(first, axis=0)
    pl.semaphore_wait(barrier, n_all - 1)
    push(ybuf.at[0], my_chan, n_chan, along_chan, 0)

    lmp[...] = jnp.zeros_like(lmp)
    lmp[0:dirs, :] = lm_ref[...]
    tbp[...] = jnp.zeros_like(tbp)
    tbp[0:dirs, :] = tb_ref[...]
    clp[...] = jnp.full_like(clp, -1)
    clp[0:1, 0:dirs] = cluster_ref[...]
    c1, c2, c3 = split3(coords_ref[...])
    coord_rows[...] = jnp.zeros_like(coord_rows)
    coord_rows[0:2, :] = c1
    coord_rows[2:4, :] = c2
    coord_rows[4:6, :] = c3
    station = lax.broadcasted_iota(jnp.int32, (stations, base_dev), 0)
    pick = jnp.where(station == pair_ref[0:1, :], F32(1.0), F32(0.0)) - jnp.where(
        station == pair_ref[1:2, :], F32(1.0), F32(0.0)
    )
    uv_ref[...] = jnp.dot(coord_rows[...].astype(BF16), pick.astype(BF16), preferred_element_type=F32)
    uv = uv_ref[0:2, :] + uv_ref[2:4, :] + uv_ref[4:6, :]
    geo = lmp[:, 0:1] * uv[0:1, :] + lmp[:, 1:2] * uv[1:2, :]
    for c in range(chan_dev):
        chan = jnp.full((1, tile), my_chan * chan_dev + c, jnp.int32).astype(F32)
        scale = F32(PHASE_SCALE) * (F32(1.0) + chan / F32(channels))
        for j in range(tiles):
            cos, sin = sincos(scale * geo[:, j * tile : (j + 1) * tile])
            resp[j, :, c * tile : (c + 1) * tile] = cos.astype(BF16)
            resp[j, :, (chan_dev + c) * tile : (chan_dev + c + 1) * tile] = sin.astype(BF16)

    def advance(block, step):
        parts = []
        for j in range(tiles):
            z1, z2, z3 = split3(block[j])
            lhs = jnp.concatenate([z1, z2, z3, jnp.zeros_like(z1)], axis=0).astype(BF16)
            p1 = jnp.dot(lhs, gsplit[j, 0], preferred_element_type=F32)
            p2 = jnp.dot(lhs, gsplit[j, 1], preferred_element_type=F32)
            p3 = jnp.dot(lhs, gsplit[j, 2], preferred_element_type=F32)
            low = p1[2 * rank : 3 * rank] + p2[rank : 2 * rank] + p3[:rank]
            parts.append(p1[:rank] + (p1[rank : 2 * rank] + p2[:rank] + low))
        ybuf[step, my_chan] = jnp.concatenate(parts, axis=0)
        push(ybuf.at[step], my_chan, n_chan, along_chan, step)

    def gathered(step):
        arrived(ybuf.at[step], n_chan, step)
        return orthonormal(total(ybuf.at[step], n_chan).reshape(tiles, rank, times))

    advance(gathered(0), 1)

    tb = tbp[...]
    beam_gram = lax.dot_general(tb, tb, NT, precision=HIGHEST, preferred_element_type=F32)
    member = jnp.where(
        lax.broadcasted_iota(jnp.int32, (LANES, dpad), 0) == clp[0:1, 0:dpad], F32(1.0), F32(0.0)
    )
    member_rows = member[0:GROUP]
    halves = []
    for j in range(tiles):
        r = resp[j]
        model = lax.dot_general(r, r, NT, preferred_element_type=F32)
        halves.append(jnp.dot(member_rows, model * beam_gram, precision=HIGHEST, preferred_element_type=F32))
    half = jnp.concatenate(halves, axis=0)
    nbuf[my_chan] = lax.dot_general(half, member, NT, precision=HIGHEST, preferred_element_type=F32)
    push(nbuf, my_chan, n_chan, along_chan, SUB_ITERS)
    before = []
    for j in range(tiles):
        bp = jnp.dot(resp[j], vis_tile(j), preferred_element_type=F32)
        before.append(jnp.sum(bp * tb, axis=-1, keepdims=True))
        b1, b2, b3 = split3(bp)
        bsplit[j, 0] = b1.astype(BF16)
        bsplit[j, 1] = b2.astype(BF16)
        bsplit[j, 2] = b3.astype(BF16)
    b1, b2, b3 = split3(tb)
    bsplit[tiles, 0] = b1.astype(BF16)
    bsplit[tiles, 1] = b2.astype(BF16)
    bsplit[tiles, 2] = b3.astype(BF16)

    advance(gathered(1), 2)

    arrived(nbuf, n_chan, SUB_ITERS)
    normal = total(nbuf, n_chan)
    sub = lax.broadcasted_iota(jnp.int32, (GROUP, LANES), 0)
    lane = lax.broadcasted_iota(jnp.int32, (GROUP, LANES), 1)
    eye = jnp.where(sub == lane, F32(1.0), F32(0.0))
    inv, inv_rho = [], []
    for j in range(tiles):
        mat = normal[j * GROUP : (j + 1) * GROUP]
        trace = jnp.sum(jnp.sum(mat * eye, axis=1, keepdims=True), axis=0, keepdims=True)
        recip = F32(1.0) / (F32(RHO_SCALE) * trace / F32(CL))
        inv_rho.append(recip)
        inv.append(mat * recip + eye)
    for p in range(CL):
        for j in range(tiles):
            mat = inv[j]
            col = mat[:, p : p + 1]
            row = mat[p : p + 1, :]
            d = F32(1.0) / mat[p : p + 1, p : p + 1]
            row = jnp.where(lane[0:1] == p, d, row * d)
            mat = jnp.where(lane == p, F32(0.0), mat)
            inv[j] = jnp.where(sub == p, row, mat - col * row)
    big, start = [], []
    for j in range(tiles):
        e = eye - inv[j]
        a = inv[j] * inv_rho[j]
        if j:
            e = pltpu.roll(e, j * GROUP, 1)
            a = pltpu.roll(a, j * GROUP, 1)
        big.append(e)
        start.append(a)
    pad = jnp.zeros((LANES - tiles * GROUP, LANES), F32)
    e1 = jnp.concatenate(big + [pad], axis=0)
    a0 = jnp.concatenate(start + [pad], axis=0)

    def times_of(a, b):
        return jnp.dot(a, b, precision=HIGHEST, preferred_element_type=F32)

    def fold(m):
        out = m[0:GROUP]
        for j in range(1, tiles):
            out = out + m[j * GROUP : (j + 1) * GROUP]
        return out

    def fold_lanes(m):
        out = m
        for j in range(1, tiles):
            out = out + pltpu.roll(m, LANES - j * GROUP, 1)
        return jnp.where(lax.broadcasted_iota(jnp.int32, m.shape, 1) < GROUP, out, F32(0.0))

    e2 = times_of(e1, e1)
    e3 = times_of(e2, e1)
    e4 = times_of(e2, e2)
    e5 = times_of(e2, e3)
    powers = [fold(m) for m in (e1, e2, e3, e4, e5)]
    packed = fold_lanes(powers[0])
    for p in range(1, ADMM_ITERS - 1):
        packed = packed + pltpu.roll(fold_lanes(powers[p]), p * GROUP, 1)
    mbuf[my_bl] = packed
    push(mbuf, my_bl, n_bl, along_bl, SUB_ITERS + 1)
    series = [a0]
    for m in (e1, e2, e3, e4, e5):
        series.append(times_of(m, a0))
    series = [fold(m) for m in series]
    eye_all = jnp.where(lax.rem(lane, GROUP) == sub, F32(1.0), F32(0.0))
    eye_all = jnp.where(lane < tiles * GROUP, eye_all, F32(0.0))
    powers = [eye_all] + powers

    basis = gathered(2).astype(BF16).astype(F32).reshape(tiles * rank, times)
    basis_ref[...] = basis
    lhs = bsplit[...].reshape((tiles + 1) * 3 * dpad, times)
    coef = lax.dot_general(lhs, basis.astype(BF16), NT, preferred_element_type=F32)

    def joined(i):
        at = i * 3 * dpad
        return coef[at : at + dpad] + (coef[at + dpad : at + 2 * dpad] + coef[at + 2 * dpad : at + 3 * dpad])

    beam_coef = joined(tiles)
    col_lane = lax.broadcasted_iota(jnp.int32, (dpad, tiles * rank), 1)
    wide_lane = lax.broadcasted_iota(jnp.int32, (dpad, LANES), 1)
    cols = jnp.zeros((dpad, LANES), F32)
    for j in range(tiles):
        inside = (col_lane >= j * rank) & (col_lane < (j + 1) * rank)
        product = jnp.where(inside, joined(j) * beam_coef, F32(0.0))
        col = before[j] - jnp.sum(product, axis=-1, keepdims=True)
        here = (wide_lane >= j * GROUP) & (wide_lane < (j + 1) * GROUP)
        cols = jnp.where(here, col, cols)
    rhs = jnp.dot(member_rows, cols, precision=HIGHEST, preferred_element_type=F32)
    rows, run = [], None
    for m in range(ADMM_ITERS):
        row = jnp.sum(series[m] * rhs, axis=0, keepdims=True)
        run = row if m == 0 else run + row
        rows.append(run)
        last = row
    out_sub = lax.broadcasted_iota(jnp.int32, (8, LANES), 0)
    block = jnp.zeros((8, LANES), F32)
    for m in range(ADMM_ITERS):
        block = jnp.where(out_sub == m, rows[m], block)
    block = fold_lanes(block)
    vbuf[my_id] = jnp.where(out_sub == ADMM_ITERS, last, block)
    push(vbuf, my_id, n_all, everyone, SUB_ITERS + 2)

    arrived(mbuf, n_bl, SUB_ITERS + 1)
    moments = total(mbuf, n_bl) * F32(1.0 / tiles_all)
    history = [eye]
    for p in range(ADMM_ITERS - 1):
        m = moments if p == 0 else pltpu.roll(moments, LANES - p * GROUP, 1)
        history.append(jnp.where(lane < GROUP, m, F32(0.0)))
    gain = [history[p] - F32(2.0) * history[p + 1] for p in range(ADMM_ITERS - 1)]
    local = []
    for i in range(1, ADMM_ITERS - 1):
        k = ADMM_ITERS - 2 - i
        local.append(F32(3.0) * powers[k + 1] - powers[k] - F32(2.0) * powers[k + 2])
    local.append(F32(2.0) * (powers[0] - powers[1]))
    arrived(vbuf, n_all, SUB_ITERS + 2)
    sums = total(vbuf, n_all) * F32(1.0 / tiles_all)
    mine = vbuf[my_bl]
    for i in range(1, n_chan):
        mine = mine + vbuf[i * n_bl + my_bl]
    x = mine[ADMM_ITERS : ADMM_ITERS + 1]
    cols_z = []
    spread = jnp.zeros((GROUP, LANES), F32)
    for k in range(ADMM_ITERS):
        z = sums[k : k + 1]
        if k:
            acc = gain[k - 1] * cols_z[0]
            for i in range(1, k):
                acc = acc + gain[k - 1 - i] * cols_z[i]
            z = z + jnp.sum(acc, axis=0, keepdims=True)
        if k < ADMM_ITERS - 1:
            col = jnp.sum(eye * z, axis=1, keepdims=True)
            cols_z.append(col)
            spread = spread + local[k] * col
    x = x + jnp.sum(spread, axis=0, keepdims=True)
    factor = F32((channels * tile * times) ** 0.5)
    x = jnp.broadcast_to(x * factor, (8, LANES))
    for j in range(tiles):
        at = x if j == 0 else pltpu.roll(x, LANES - j * GROUP, 1)
        gains_ref[j : j + 1, :] = at[0:1, 0:CL]
    cons_ref[...] = (z * factor)[:, 0:CL]

    for step in range(SUB_ITERS):
        sent(ybuf.at[step], n_chan, step)
    sent(nbuf, n_chan, SUB_ITERS)
    sent(mbuf, n_bl, SUB_ITERS + 1)
    sent(vbuf, n_all, SUB_ITERS + 2)


def clean_kernel(vis_ref, basis_ref, out_ref):
    rank = basis_ref.shape[0]
    times = basis_ref.shape[1]
    basis = basis_ref[...]
    wide = jnp.concatenate([basis, basis, basis, jnp.zeros_like(basis)], axis=0).astype(BF16)
    v = vis_ref[...].reshape(-1, times)
    proj = lax.dot_general(v, wide, NT, preferred_element_type=F32)
    lane = lax.broadcasted_iota(jnp.int32, (1, 4 * rank), 1)
    a, b, c = split3(proj)
    parts = jnp.where(lane < rank, a, jnp.where(lane < 2 * rank, b, c)).astype(BF16)
    correction = jnp.dot(parts, wide, preferred_element_type=F32)
    out_ref[...] = (v.astype(F32) - correction).astype(BF16).reshape(out_ref.shape)


def per_device(vis, station_pair_index, station_coords, dir_lm, time_beam, dir_cluster, seed_block):
    n_chan = lax.axis_size("chan")
    n_bl = lax.axis_size("bl")
    chan_dev, base_dev, times = vis.shape[1:]
    tiles, _, rank = seed_block.shape
    tile = base_dev // tiles
    dirs = dir_lm.shape[0]
    dpad = (dirs + 15) // 16 * 16
    stations = station_coords.shape[0]
    vmem = pl.BlockSpec(memory_space=pltpu.VMEM)
    basis, gains, consensus = pl.pallas_call(
        functools.partial(main_kernel, n_chan, n_bl, chan_dev * n_chan),
        out_shape=(
            jax.ShapeDtypeStruct((tiles * rank, times), F32),
            jax.ShapeDtypeStruct((tiles, CL), F32),
            jax.ShapeDtypeStruct((1, CL), F32),
        ),
        in_specs=[vmem] * 7,
        out_specs=(vmem,) * 3,
        scratch_shapes=[
            pltpu.VMEM((tiles, 3, times, times), BF16),
            pltpu.VMEM((tiles, dpad, 2 * chan_dev * tile), BF16),
            pltpu.VMEM((dpad, 2), F32),
            pltpu.VMEM((dpad, times), F32),
            pltpu.VMEM((8, LANES), jnp.int32),
            pltpu.VMEM((GROUP, stations), F32),
            pltpu.VMEM((GROUP, base_dev), F32),
            pltpu.VMEM((8, LANES), F32),
            pltpu.VMEM((tiles + 1, 3, dpad, times), BF16),
            pltpu.VMEM((SUB_ITERS, n_chan, tiles * rank, times), F32),
            pltpu.VMEM((n_chan, tiles * GROUP, LANES), F32),
            pltpu.VMEM((n_bl, GROUP, LANES), F32),
            pltpu.VMEM((n_chan * n_bl, 8, LANES), F32),
            pltpu.SemaphoreType.DMA((SUB_ITERS + 3,)),
            pltpu.SemaphoreType.DMA((SUB_ITERS + 3,)),
        ],
        compiler_params=pltpu.CompilerParams(
            collective_id=0, has_side_effects=True, vmem_limit_bytes=48 * 1024 * 1024
        ),
    )(
        vis,
        station_pair_index.T,
        station_coords.T,
        dir_lm,
        time_beam,
        dir_cluster.reshape(1, dirs),
        jnp.swapaxes(seed_block, 1, 2),
    )
    spec = pl.BlockSpec((2, chan_dev, tile, times), lambda j: (0, 0, j, 0))
    clean = pl.pallas_call(
        clean_kernel,
        grid=(tiles,),
        out_shape=jax.ShapeDtypeStruct(vis.shape, BF16),
        in_specs=[spec, pl.BlockSpec((rank, times), lambda j: (j, 0))],
        out_specs=spec,
        compiler_params=pltpu.CompilerParams(vmem_limit_bytes=32 * 1024 * 1024),
    )(vis, basis)
    return clean, gains, consensus.reshape(CL)


def solution(mesh):
    placed = (P(None, "chan", "bl", None), P("bl", None), P(), P(), P(), P(), P("bl", None, None))
    return jax.shard_map(
        per_device,
        mesh=mesh,
        in_specs=placed,
        out_specs=(P(None, "chan", "bl", None), P("bl", None), P()),
        check_vma=False,
    )
```

```python
import functools

import jax
import jax.numpy as jnp
from jax import lax
from jax.experimental import pallas as pl
from jax.experimental.pallas import tpu as pltpu
from jax.sharding import PartitionSpec as P

CL = 12
SUB_ITERS = 3
ADMM_ITERS = 6
PHASE_SCALE = 20.0
RHO_SCALE = 0.5

HIGHEST = lax.Precision.HIGHEST
MESH = pl.DeviceIdType.MESH
F32 = jnp.float32
BF16 = jnp.bfloat16
LANES = 128
GROUP = 16
NT = (((1,), (1,)), ((), ()))
TN = (((0,), (0,)), ((), ()))


def split3(x):
    a = x.astype(BF16).astype(F32)
    rest = x - a
    b = rest.astype(BF16).astype(F32)
    return a, b, rest - b


def sincos(phase):
    k = jnp.floor(phase * F32(0.6366197723675814) + F32(0.5))
    r = phase - k * F32(1.5703125)
    r = r - k * F32(4.837512969970703125e-4)
    r = r - k * F32(7.54978995489188216e-8)
    r2 = r * r
    s = r + r * r2 * (F32(-1.6666654611e-1) + r2 * (F32(8.3321608736e-3) + r2 * F32(-1.9515295891e-4)))
    c = (F32(1.0) - F32(0.5) * r2) + r2 * r2 * (
        F32(4.166664568298827e-2) + r2 * (F32(-1.388731625493765e-3) + r2 * F32(2.443315711809948e-5))
    )
    ki = k.astype(jnp.int32)
    odd = (ki & 1) == 1
    cos = jnp.where(odd, s, c)
    sin = jnp.where(odd, c, s)
    cos = jnp.where(((ki + 1) & 2) == 2, -cos, cos)
    sin = jnp.where((ki & 2) == 2, -sin, sin)
    return cos, sin


def orthonormal(rows):
    sub = lax.broadcasted_iota(jnp.int32, (1, rows.shape[1], 1), 1)
    for k in range(rows.shape[1]):
        lead = rows[:, k : k + 1, :]
        dots = jnp.sum(rows * lead, axis=-1, keepdims=True)
        if k + 1 < rows.shape[1]:
            coef = jnp.where(sub > k, dots / dots[:, k : k + 1, :], F32(0.0))
            rows = rows - coef * lead
    norm = jnp.sum(rows * rows, axis=-1, keepdims=True)
    return rows / jnp.sqrt(norm)


def main_kernel(
    n_chan, n_bl, channels,
    vis_hbm, pair_hbm, coords_hbm, lm_hbm, tb_hbm, cluster_hbm, seed_hbm,
    basis_ref, gains_ref, cons_ref,
    vis_ref, pair_ref, coords_ref, lm_ref, tb_ref, cluster_ref, seed_ref,
    gsplit, resp, lmp, tbp, clp, coord_rows, uv_ref, bsplit,
    ybuf, nbuf, mbuf, vbuf, send_sems, recv_sems, vis_sems, load_sems,
):
    chan_dev, base_dev, times = vis_ref.shape[1:]
    tiles, rank = seed_ref.shape[0], seed_ref.shape[1]
    tile = base_dev // tiles
    dirs = tb_ref.shape[0]
    dpad = tbp.shape[0]
    stations = coords_ref.shape[1]
    n_all = n_chan * n_bl
    tiles_all = tiles * n_bl
    my_chan = lax.axis_index("chan")
    my_bl = lax.axis_index("bl")
    my_id = my_chan * n_bl + my_bl

    loads = [
        pltpu.make_async_copy(src, dst, load_sems.at[i])
        for i, (src, dst) in enumerate(
            (
                (seed_hbm, seed_ref),
                (pair_hbm, pair_ref),
                (coords_hbm, coords_ref),
                (lm_hbm, lm_ref),
                (tb_hbm, tb_ref),
                (cluster_hbm, cluster_ref),
            )
        )
    ]
    vis_loads = []
    for j in range(tiles):
        at = (slice(None), slice(None), pl.ds(j * tile, tile), slice(None))
        vis_loads.append(pltpu.make_async_copy(vis_hbm.at[at], vis_ref.at[at], vis_sems.at[j]))
    loads[0].start()
    for load in vis_loads:
        load.start()
    for load in loads[1:]:
        load.start()

    def everyone(off):
        other = lax.rem(my_id + off, n_all)
        return (lax.div(other, n_bl), lax.rem(other, n_bl))

    def along_chan(off):
        return (lax.rem(my_chan + off, n_chan), my_bl)

    def along_bl(off):
        return (my_chan, lax.rem(my_bl + off, n_bl))

    barrier = pltpu.get_barrier_semaphore()

    @pl.loop(1, n_all)
    def _(off):
        pl.semaphore_signal(barrier, inc=1, device_id=everyone(off), device_id_type=MESH)

    def push(buf, me, n, peer, phase):
        @pl.loop(1, n)
        def _(off):
            pltpu.make_async_remote_copy(
                src_ref=buf.at[me],
                dst_ref=buf.at[me],
                send_sem=send_sems.at[phase],
                recv_sem=recv_sems.at[phase],
                device_id=peer(off),
                device_id_type=MESH,
            ).start()

    def arrived(buf, n, phase):
        part = buf.at[pl.ds(0, n - 1)]
        pltpu.make_async_copy(part, part, recv_sems.at[phase]).wait()

    def sent(buf, n, phase):
        part = buf.at[pl.ds(0, n - 1)]
        pltpu.make_async_copy(part, part, send_sems.at[phase]).wait()

    def total(buf, n):
        out = buf[0]
        for i in range(1, n):
            out = out + buf[i]
        return out

    def vis_tile(j):
        return vis_ref[:, :, j * tile : (j + 1) * tile, :].reshape(2 * chan_dev * tile, times)

    first = []
    loads[0].wait()
    for j in range(tiles):
        vis_loads[j].wait()
        v = vis_tile(j)
        gram = lax.dot_general(v, v, TN, preferred_element_type=F32)
        g1, g2, g3 = split3(gram)
        gsplit[j, 0] = g1.astype(BF16)
        gsplit[j, 1] = g2.astype(BF16)
        gsplit[j, 2] = g3.astype(BF16)
        seed = seed_ref[j].astype(F32)
        lhs = jnp.concatenate([seed, jnp.zeros_like(seed)], axis=0).astype(BF16)
        acc = jnp.dot(lhs, gsplit[j, 2], preferred_element_type=F32)
        acc = acc + jnp.dot(lhs, gsplit[j, 1], preferred_element_type=F32)
        acc = acc + jnp.dot(lhs, gsplit[j, 0], preferred_element_type=F32)
        first.append(acc[:rank])
    ybuf[0, my_chan] = jnp.concatenate(first, axis=0)
    pl.semaphore_wait(barrier, n_all - 1)
    push(ybuf.at[0], my_chan, n_chan, along_chan, 0)

    for load in loads[1:]:
        load.wait()
    lmp[...] = jnp.zeros_like(lmp)
    lmp[0:2, 0:dirs] = lm_ref[...]
    tbp[...] = jnp.zeros_like(tbp)
    tbp[0:dirs, :] = tb_ref[...]
    clp[...] = jnp.full_like(clp, -1)
    clp[0:1, 0:dirs] = cluster_ref[...]
    c1, c2, c3 = split3(coords_ref[...])
    coord_rows[...] = jnp.zeros_like(coord_rows)
    coord_rows[0:2, :] = c1
    coord_rows[2:4, :] = c2
    coord_rows[4:6, :] = c3
    station = lax.broadcasted_iota(jnp.int32, (stations, base_dev), 0)
    pick = jnp.where(station == pair_ref[0:1, :], F32(1.0), F32(0.0)) - jnp.where(
        station == pair_ref[1:2, :], F32(1.0), F32(0.0)
    )
    uv_ref[...] = jnp.dot(coord_rows[...].astype(BF16), pick.astype(BF16), preferred_element_type=F32)
    uv = uv_ref[0:2, :] + uv_ref[2:4, :] + uv_ref[4:6, :]
    uv_ref[0:2, :] = uv
    uv_ref[2:8, :] = jnp.zeros((6, base_dev), F32)
    geo = lax.dot_general(
        lmp[:, 0:dpad], uv_ref[0:8, :], TN, precision=HIGHEST, preferred_element_type=F32
    )
    for c in range(chan_dev):
        chan = jnp.full((1, tile), my_chan * chan_dev + c, jnp.int32).astype(F32)
        scale = F32(PHASE_SCALE) * (F32(1.0) + chan / F32(channels))
        for j in range(tiles):
            cos, sin = sincos(scale * geo[:, j * tile : (j + 1) * tile])
            resp[j, :, c * tile : (c + 1) * tile] = cos.astype(BF16)
            resp[j, :, (chan_dev + c) * tile : (chan_dev + c + 1) * tile] = sin.astype(BF16)

    def advance(block, step):
        parts = []
        for j in range(tiles):
            z1, z2, z3 = split3(block[j])
            lhs = jnp.concatenate([z1, z2, z3, jnp.zeros_like(z1)], axis=0).astype(BF16)
            p1 = jnp.dot(lhs, gsplit[j, 0], preferred_element_type=F32)
            p2 = jnp.dot(lhs, gsplit[j, 1], preferred_element_type=F32)
            p3 = jnp.dot(lhs, gsplit[j, 2], preferred_element_type=F32)
            low = p1[2 * rank : 3 * rank] + p2[rank : 2 * rank] + p3[:rank]
            parts.append(p1[:rank] + (p1[rank : 2 * rank] + p2[:rank] + low))
        ybuf[step, my_chan] = jnp.concatenate(parts, axis=0)
        push(ybuf.at[step], my_chan, n_chan, along_chan, step)

    def gathered(step):
        arrived(ybuf.at[step], n_chan, step)
        return orthonormal(total(ybuf.at[step], n_chan).reshape(tiles, rank, times))

    advance(gathered(0), 1)

    tb = tbp[...]
    beam_gram = lax.dot_general(tb, tb, NT, precision=HIGHEST, preferred_element_type=F32)
    member = jnp.where(
        lax.broadcasted_iota(jnp.int32, (LANES, dpad), 0) == clp[0:1, 0:dpad], F32(1.0), F32(0.0)
    )
    member_rows = member[0:GROUP]
    halves = []
    for j in range(tiles):
        r = resp[j]
        model = lax.dot_general(r, r, NT, preferred_element_type=F32)
        halves.append(jnp.dot(member_rows, model * beam_gram, precision=HIGHEST, preferred_element_type=F32))
    half = jnp.concatenate(halves, axis=0)
    nbuf[my_chan] = lax.dot_general(half, member, NT, precision=HIGHEST, preferred_element_type=F32)
    push(nbuf, my_chan, n_chan, along_chan, SUB_ITERS)
    before = []
    for j in range(tiles):
        bp = jnp.dot(resp[j], vis_tile(j), preferred_element_type=F32)
        before.append(jnp.sum(bp * tb, axis=-1, keepdims=True))
        b1, b2, b3 = split3(bp)
        bsplit[j, 0] = b1.astype(BF16)
        bsplit[j, 1] = b2.astype(BF16)
        bsplit[j, 2] = b3.astype(BF16)
    b1, b2, b3 = split3(tb)
    bsplit[tiles, 0] = b1.astype(BF16)
    bsplit[tiles, 1] = b2.astype(BF16)
    bsplit[tiles, 2] = b3.astype(BF16)

    advance(gathered(1), 2)

    arrived(nbuf, n_chan, SUB_ITERS)
    normal = total(nbuf, n_chan)
    sub = lax.broadcasted_iota(jnp.int32, (GROUP, LANES), 0)
    lane = lax.broadcasted_iota(jnp.int32, (GROUP, LANES), 1)
    eye = jnp.where(sub == lane, F32(1.0), F32(0.0))
    inv, inv_rho = [], []
    for j in range(tiles):
        mat = normal[j * GROUP : (j + 1) * GROUP]
        trace = jnp.sum(jnp.sum(mat * eye, axis=1, keepdims=True), axis=0, keepdims=True)
        recip = F32(1.0) / (F32(RHO_SCALE) * trace / F32(CL))
        inv_rho.append(recip)
        inv.append(mat * recip + eye)
    for p in range(CL):
        for j in range(tiles):
            mat = inv[j]
            col = mat[:, p : p + 1]
            row = mat[p : p + 1, :]
            d = F32(1.0) / mat[p : p + 1, p : p + 1]
            row = jnp.where(lane[0:1] == p, d, row * d)
            mat = jnp.where(lane == p, F32(0.0), mat)
            inv[j] = jnp.where(sub == p, row, mat - col * row)
    big, start = [], []
    for j in range(tiles):
        e = eye - inv[j]
        a = inv[j] * inv_rho[j]
        if j:
            e = pltpu.roll(e, j * GROUP, 1)
            a = pltpu.roll(a, j * GROUP, 1)
        big.append(e)
        start.append(a)
    pad = jnp.zeros((LANES - tiles * GROUP, LANES), F32)
    e1 = jnp.concatenate(big + [pad], axis=0)
    a0 = jnp.concatenate(start + [pad], axis=0)

    def times_of(a, b):
        return jnp.dot(a, b, precision=HIGHEST, preferred_element_type=F32)

    def fold(m):
        out = m[0:GROUP]
        for j in range(1, tiles):
            out = out + m[j * GROUP : (j + 1) * GROUP]
        return out

    def fold_lanes(m):
        out = m
        for j in range(1, tiles):
            out = out + pltpu.roll(m, LANES - j * GROUP, 1)
        return jnp.where(lax.broadcasted_iota(jnp.int32, m.shape, 1) < GROUP, out, F32(0.0))

    e2 = times_of(e1, e1)
    e3 = times_of(e2, e1)
    e4 = times_of(e2, e2)
    e5 = times_of(e2, e3)
    powers = [fold(m) for m in (e1, e2, e3, e4, e5)]
    packed = fold_lanes(powers[0])
    for p in range(1, ADMM_ITERS - 1):
        packed = packed + pltpu.roll(fold_lanes(powers[p]), p * GROUP, 1)
    mbuf[my_bl] = packed
    push(mbuf, my_bl, n_bl, along_bl, SUB_ITERS + 1)
    series = [a0]
    for m in (e1, e2, e3, e4, e5):
        series.append(times_of(m, a0))
    series = [fold(m) for m in series]
    eye_all = jnp.where(lax.rem(lane, GROUP) == sub, F32(1.0), F32(0.0))
    eye_all = jnp.where(lane < tiles * GROUP, eye_all, F32(0.0))
    powers = [eye_all] + powers

    basis = gathered(2).astype(BF16).astype(F32).reshape(tiles * rank, times)
    basis_ref[...] = basis
    lhs = bsplit[...].reshape((tiles + 1) * 3 * dpad, times)
    coef = lax.dot_general(lhs, basis.astype(BF16), NT, preferred_element_type=F32)

    def joined(i):
        at = i * 3 * dpad
        return coef[at : at + dpad] + (coef[at + dpad : at + 2 * dpad] + coef[at + 2 * dpad : at + 3 * dpad])

    beam_coef = joined(tiles)
    col_lane = lax.broadcasted_iota(jnp.int32, (dpad, tiles * rank), 1)
    wide_lane = lax.broadcasted_iota(jnp.int32, (dpad, LANES), 1)
    cols = jnp.zeros((dpad, LANES), F32)
    for j in range(tiles):
        inside = (col_lane >= j * rank) & (col_lane < (j + 1) * rank)
        product = jnp.where(inside, joined(j) * beam_coef, F32(0.0))
        col = before[j] - jnp.sum(product, axis=-1, keepdims=True)
        here = (wide_lane >= j * GROUP) & (wide_lane < (j + 1) * GROUP)
        cols = jnp.where(here, col, cols)
    rhs = jnp.dot(member_rows, cols, precision=HIGHEST, preferred_element_type=F32)
    rows, run = [], None
    for m in range(ADMM_ITERS):
        row = jnp.sum(series[m] * rhs, axis=0, keepdims=True)
        run = row if m == 0 else run + row
        rows.append(run)
        last = row
    out_sub = lax.broadcasted_iota(jnp.int32, (8, LANES), 0)
    block = jnp.zeros((8, LANES), F32)
    for m in range(ADMM_ITERS):
        block = jnp.where(out_sub == m, rows[m], block)
    block = fold_lanes(block)
    vbuf[my_id] = jnp.where(out_sub == ADMM_ITERS, last, block)
    push(vbuf, my_id, n_all, everyone, SUB_ITERS + 2)

    arrived(mbuf, n_bl, SUB_ITERS + 1)
    moments = total(mbuf, n_bl) * F32(1.0 / tiles_all)
    history = [eye]
    for p in range(ADMM_ITERS - 1):
        m = moments if p == 0 else pltpu.roll(moments, LANES - p * GROUP, 1)
        history.append(jnp.where(lane < GROUP, m, F32(0.0)))
    gain = [history[p] - F32(2.0) * history[p + 1] for p in range(ADMM_ITERS - 1)]
    local = []
    for i in range(1, ADMM_ITERS - 1):
        k = ADMM_ITERS - 2 - i
        local.append(F32(3.0) * powers[k + 1] - powers[k] - F32(2.0) * powers[k + 2])
    local.append(F32(2.0) * (powers[0] - powers[1]))
    arrived(vbuf, n_all, SUB_ITERS + 2)
    sums = total(vbuf, n_all) * F32(1.0 / tiles_all)
    mine = vbuf[my_bl]
    for i in range(1, n_chan):
        mine = mine + vbuf[i * n_bl + my_bl]
    x = mine[ADMM_ITERS : ADMM_ITERS + 1]
    cols_z = []
    spread = jnp.zeros((GROUP, LANES), F32)
    for k in range(ADMM_ITERS):
        z = sums[k : k + 1]
        if k:
            acc = gain[k - 1] * cols_z[0]
            for i in range(1, k):
                acc = acc + gain[k - 1 - i] * cols_z[i]
            z = z + jnp.sum(acc, axis=0, keepdims=True)
        if k < ADMM_ITERS - 1:
            col = jnp.sum(eye * z, axis=1, keepdims=True)
            cols_z.append(col)
            spread = spread + local[k] * col
    x = x + jnp.sum(spread, axis=0, keepdims=True)
    factor = F32((channels * tile * times) ** 0.5)
    x = jnp.broadcast_to(x * factor, (8, LANES))
    for j in range(tiles):
        at = x if j == 0 else pltpu.roll(x, LANES - j * GROUP, 1)
        gains_ref[j : j + 1, :] = at[0:1, 0:CL]
    cons_ref[...] = (z * factor)[:, 0:CL]

    for step in range(SUB_ITERS):
        sent(ybuf.at[step], n_chan, step)
    sent(nbuf, n_chan, SUB_ITERS)
    sent(mbuf, n_bl, SUB_ITERS + 1)
    sent(vbuf, n_all, SUB_ITERS + 2)


def clean_kernel(vis_ref, basis_ref, gains_in, cons_in, out_ref, gains_ref, cons_ref):
    gains_ref[...] = gains_in[...]
    cons_ref[...] = cons_in[...]
    rank = basis_ref.shape[0]
    times = basis_ref.shape[1]
    basis = basis_ref[...]
    wide = jnp.concatenate([basis, basis, basis, jnp.zeros_like(basis)], axis=0).astype(BF16)
    v = vis_ref[...].reshape(-1, times)
    proj = lax.dot_general(v, wide, NT, preferred_element_type=F32)
    lane = lax.broadcasted_iota(jnp.int32, (1, 4 * rank), 1)
    a, b, c = split3(proj)
    parts = jnp.where(lane < rank, a, jnp.where(lane < 2 * rank, b, c)).astype(BF16)
    correction = jnp.dot(parts, wide, preferred_element_type=F32)
    out_ref[...] = (v.astype(F32) - correction).astype(BF16).reshape(out_ref.shape)


def per_device(vis, station_pair_index, station_coords, dir_lm, time_beam, dir_cluster, seed_block):
    n_chan = lax.axis_size("chan")
    n_bl = lax.axis_size("bl")
    chan_dev, base_dev, times = vis.shape[1:]
    tiles, _, rank = seed_block.shape
    tile = base_dev // tiles
    dirs = dir_lm.shape[0]
    dpad = (dirs + 15) // 16 * 16
    stations = station_coords.shape[0]
    vmem = pl.BlockSpec(memory_space=pltpu.VMEM)
    basis, gains, consensus = pl.pallas_call(
        functools.partial(main_kernel, n_chan, n_bl, chan_dev * n_chan),
        out_shape=(
            jax.ShapeDtypeStruct((tiles * rank, times), F32),
            jax.ShapeDtypeStruct((tiles, CL), F32),
            jax.ShapeDtypeStruct((1, CL), F32),
        ),
        in_specs=[pl.BlockSpec(memory_space=pl.ANY)] * 7,
        out_specs=(vmem,) * 3,
        scratch_shapes=[
            pltpu.VMEM(vis.shape, BF16),
            pltpu.VMEM((2, base_dev), jnp.int32),
            pltpu.VMEM((2, stations), F32),
            pltpu.VMEM((2, dirs), F32),
            pltpu.VMEM((dirs, times), F32),
            pltpu.VMEM((1, dirs), jnp.int32),
            pltpu.VMEM((tiles, rank, times), jnp.int32),
            pltpu.VMEM((tiles, 3, times, times), BF16),
            pltpu.VMEM((tiles, dpad, 2 * chan_dev * tile), BF16),
            pltpu.VMEM((8, LANES), F32),
            pltpu.VMEM((dpad, times), F32),
            pltpu.VMEM((8, LANES), jnp.int32),
            pltpu.VMEM((GROUP, stations), F32),
            pltpu.VMEM((GROUP, base_dev), F32),
            pltpu.VMEM((tiles + 1, 3, dpad, times), BF16),
            pltpu.VMEM((SUB_ITERS, n_chan, tiles * rank, times), F32),
            pltpu.VMEM((n_chan, tiles * GROUP, LANES), F32),
            pltpu.VMEM((n_bl, GROUP, LANES), F32),
            pltpu.VMEM((n_chan * n_bl, 8, LANES), F32),
            pltpu.SemaphoreType.DMA((SUB_ITERS + 3,)),
            pltpu.SemaphoreType.DMA((SUB_ITERS + 3,)),
            pltpu.SemaphoreType.DMA((tiles,)),
            pltpu.SemaphoreType.DMA((6,)),
        ],
        compiler_params=pltpu.CompilerParams(
            collective_id=0, has_side_effects=True, vmem_limit_bytes=60 * 1024 * 1024
        ),
    )(
        vis,
        station_pair_index.T,
        station_coords.T,
        dir_lm.T,
        time_beam,
        dir_cluster.reshape(1, dirs),
        jnp.swapaxes(seed_block, 1, 2),
    )
    spec = pl.BlockSpec((2, chan_dev, tile, times), lambda j: (0, 0, j, 0))
    gains_spec = pl.BlockSpec((tiles, CL), lambda j: (0, 0))
    cons_spec = pl.BlockSpec((1, CL), lambda j: (0, 0))
    clean, gains, consensus = pl.pallas_call(
        clean_kernel,
        grid=(tiles,),
        out_shape=(
            jax.ShapeDtypeStruct(vis.shape, BF16),
            jax.ShapeDtypeStruct((tiles, CL), F32),
            jax.ShapeDtypeStruct((1, CL), F32),
        ),
        in_specs=[spec, pl.BlockSpec((rank, times), lambda j: (j, 0)), gains_spec, cons_spec],
        out_specs=(spec, gains_spec, cons_spec),
        compiler_params=pltpu.CompilerParams(vmem_limit_bytes=60 * 1024 * 1024),
    )(vis, basis, gains, consensus)
    return clean, gains, consensus.reshape(CL)


def solution(mesh):
    placed = (P(None, "chan", "bl", None), P("bl", None), P(), P(), P(), P(), P("bl", None, None))
    return jax.shard_map(
        per_device,
        mesh=mesh,
        in_specs=placed,
        out_specs=(P(None, "chan", "bl", None), P("bl", None), P()),
        check_vma=False,
    )
```

```python
import functools

import jax
import jax.numpy as jnp
from jax import lax
from jax.experimental import pallas as pl
from jax.experimental.pallas import tpu as pltpu
from jax.sharding import PartitionSpec as P

CL = 12
SUB_ITERS = 3
ADMM_ITERS = 6
PHASE_SCALE = 20.0
RHO_SCALE = 0.5

HIGHEST = lax.Precision.HIGHEST
MESH = pl.DeviceIdType.MESH
F32 = jnp.float32
BF16 = jnp.bfloat16
LANES = 128
GROUP = 16
NT = (((1,), (1,)), ((), ()))
TN = (((0,), (0,)), ((), ()))


def split3(x):
    a = x.astype(BF16).astype(F32)
    rest = x - a
    b = rest.astype(BF16).astype(F32)
    return a, b, rest - b


def sincos(phase):
    k = jnp.floor(phase * F32(0.6366197723675814) + F32(0.5))
    r = phase - k * F32(1.5703125)
    r = r - k * F32(4.837512969970703125e-4)
    r = r - k * F32(7.54978995489188216e-8)
    r2 = r * r
    s = r + r * r2 * (F32(-1.6666654611e-1) + r2 * (F32(8.3321608736e-3) + r2 * F32(-1.9515295891e-4)))
    c = (F32(1.0) - F32(0.5) * r2) + r2 * r2 * (
        F32(4.166664568298827e-2) + r2 * (F32(-1.388731625493765e-3) + r2 * F32(2.443315711809948e-5))
    )
    ki = k.astype(jnp.int32)
    odd = (ki & 1) == 1
    cos = jnp.where(odd, s, c)
    sin = jnp.where(odd, c, s)
    cos = jnp.where(((ki + 1) & 2) == 2, -cos, cos)
    sin = jnp.where((ki & 2) == 2, -sin, sin)
    return cos, sin


def orthonormal(rows):
    count = rows.shape[1]
    sub = lax.broadcasted_iota(jnp.int32, (1, count, 1), 1)
    for k in range(0, count, 2):
        lead = rows[:, k : k + 1, :]
        follow = rows[:, k + 1 : k + 2, :]
        dots = jnp.sum(rows * lead, axis=-1, keepdims=True)
        others = jnp.sum(rows * follow, axis=-1, keepdims=True)
        ratio = dots / dots[:, k : k + 1, :]
        mix = ratio[:, k + 1 : k + 2, :]
        follow = follow - mix * lead
        others = others - mix * dots
        coef = jnp.where(sub > k, ratio, F32(0.0))
        coef_follow = jnp.where(sub > k + 1, others / others[:, k + 1 : k + 2, :], F32(0.0))
        rows = rows - coef * lead - coef_follow * follow
    norm = jnp.sum(rows * rows, axis=-1, keepdims=True)
    return rows / jnp.sqrt(norm)


def main_kernel(
    n_chan, n_bl, channels,
    vis_hbm, pair_hbm, coords_hbm, lm_hbm, tb_hbm, cluster_hbm, seed_hbm,
    clean_hbm, gains_ref, cons_ref,
    clean_ref, vis_ref, pair_ref, coords_ref, lm_ref, tb_ref, cluster_ref, seed_ref,
    gsplit, resp, lmp, tbp, clp, coord_rows, uv_ref, bsplit,
    ybuf, nbuf, mbuf, vbuf, send_sems, recv_sems, vis_sems, load_sems, clean_sems,
):
    chan_dev, base_dev, times = vis_ref.shape[1:]
    tiles, rank = seed_ref.shape[0], seed_ref.shape[1]
    tile = base_dev // tiles
    dirs = tb_ref.shape[0]
    dpad = tbp.shape[0]
    stations = coords_ref.shape[1]
    n_all = n_chan * n_bl
    tiles_all = tiles * n_bl
    my_chan = lax.axis_index("chan")
    my_bl = lax.axis_index("bl")
    my_id = my_chan * n_bl + my_bl

    loads = [
        pltpu.make_async_copy(src, dst, load_sems.at[i])
        for i, (src, dst) in enumerate(
            (
                (seed_hbm, seed_ref),
                (pair_hbm, pair_ref),
                (coords_hbm, coords_ref),
                (lm_hbm, lm_ref),
                (tb_hbm, tb_ref),
                (cluster_hbm, cluster_ref),
            )
        )
    ]
    vis_loads = []
    for j in range(tiles):
        at = (slice(None), slice(None), pl.ds(j * tile, tile), slice(None))
        vis_loads.append(pltpu.make_async_copy(vis_hbm.at[at], vis_ref.at[at], vis_sems.at[j]))
    loads[0].start()
    for load in vis_loads:
        load.start()
    for load in loads[1:]:
        load.start()

    def everyone(off):
        other = lax.rem(my_id + off, n_all)
        return (lax.div(other, n_bl), lax.rem(other, n_bl))

    def along_chan(off):
        return (lax.rem(my_chan + off, n_chan), my_bl)

    def along_bl(off):
        return (my_chan, lax.rem(my_bl + off, n_bl))

    barrier = pltpu.get_barrier_semaphore()

    @pl.loop(1, n_all)
    def _(off):
        pl.semaphore_signal(barrier, inc=1, device_id=everyone(off), device_id_type=MESH)

    def push(buf, me, n, peer, phase):
        @pl.loop(1, n)
        def _(off):
            pltpu.make_async_remote_copy(
                src_ref=buf.at[me],
                dst_ref=buf.at[me],
                send_sem=send_sems.at[phase],
                recv_sem=recv_sems.at[phase],
                device_id=peer(off),
                device_id_type=MESH,
            ).start()

    def arrived(buf, n, phase):
        part = buf.at[pl.ds(0, n - 1)]
        pltpu.make_async_copy(part, part, recv_sems.at[phase]).wait()

    def sent(buf, n, phase):
        part = buf.at[pl.ds(0, n - 1)]
        pltpu.make_async_copy(part, part, send_sems.at[phase]).wait()

    def total(buf, n):
        out = buf[0]
        for i in range(1, n):
            out = out + buf[i]
        return out

    def vis_tile(j):
        return vis_ref[:, :, j * tile : (j + 1) * tile, :].reshape(2 * chan_dev * tile, times)

    first = []
    loads[0].wait()
    for j in range(tiles):
        vis_loads[j].wait()
        v = vis_tile(j)
        gram = lax.dot_general(v, v, TN, preferred_element_type=F32)
        g1, g2, g3 = split3(gram)
        gsplit[j, 0] = g1.astype(BF16)
        gsplit[j, 1] = g2.astype(BF16)
        gsplit[j, 2] = g3.astype(BF16)
        seed = seed_ref[j].astype(F32)
        lhs = jnp.concatenate([seed, jnp.zeros_like(seed)], axis=0).astype(BF16)
        acc = jnp.dot(lhs, gsplit[j, 2], preferred_element_type=F32)
        acc = acc + jnp.dot(lhs, gsplit[j, 1], preferred_element_type=F32)
        acc = acc + jnp.dot(lhs, gsplit[j, 0], preferred_element_type=F32)
        first.append(acc[:rank])
    ybuf[0, my_chan] = jnp.concatenate(first, axis=0)
    pl.semaphore_wait(barrier, n_all - 1)
    push(ybuf.at[0], my_chan, n_chan, along_chan, 0)

    for load in loads[1:]:
        load.wait()
    lmp[...] = jnp.zeros_like(lmp)
    lmp[0:2, 0:dirs] = lm_ref[...]
    tbp[...] = jnp.zeros_like(tbp)
    tbp[0:dirs, :] = tb_ref[...]
    clp[...] = jnp.full_like(clp, -1)
    clp[0:1, 0:dirs] = cluster_ref[...]
    c1, c2, c3 = split3(coords_ref[...])
    coord_rows[...] = jnp.zeros_like(coord_rows)
    coord_rows[0:2, :] = c1
    coord_rows[2:4, :] = c2
    coord_rows[4:6, :] = c3
    tb = tbp[...]
    beam_gram = lax.dot_general(tb, tb, NT, precision=HIGHEST, preferred_element_type=F32)
    member = jnp.where(
        lax.broadcasted_iota(jnp.int32, (LANES, dpad), 0) == clp[0:1, 0:dpad], F32(1.0), F32(0.0)
    )
    station = lax.broadcasted_iota(jnp.int32, (stations, base_dev), 0)
    pick = jnp.where(station == pair_ref[0:1, :], F32(1.0), F32(0.0)) - jnp.where(
        station == pair_ref[1:2, :], F32(1.0), F32(0.0)
    )
    uv_ref[...] = jnp.dot(coord_rows[...].astype(BF16), pick.astype(BF16), preferred_element_type=F32)
    uv = uv_ref[0:2, :] + uv_ref[2:4, :] + uv_ref[4:6, :]
    uv_ref[0:2, :] = uv
    uv_ref[2:8, :] = jnp.zeros((6, base_dev), F32)
    geo = lax.dot_general(
        lmp[:, 0:dpad], uv_ref[0:8, :], TN, precision=HIGHEST, preferred_element_type=F32
    )
    for c in range(chan_dev):
        chan = jnp.full((1, tile), my_chan * chan_dev + c, jnp.int32).astype(F32)
        scale = F32(PHASE_SCALE) * (F32(1.0) + chan / F32(channels))
        for j in range(tiles):
            cos, sin = sincos(scale * geo[:, j * tile : (j + 1) * tile])
            resp[j, :, c * tile : (c + 1) * tile] = cos.astype(BF16)
            resp[j, :, (chan_dev + c) * tile : (chan_dev + c + 1) * tile] = sin.astype(BF16)

    def advance(block, step):
        parts = []
        for j in range(tiles):
            z1, z2, z3 = split3(block[j])
            lhs = jnp.concatenate([z1, z2, z3, jnp.zeros_like(z1)], axis=0).astype(BF16)
            p1 = jnp.dot(lhs, gsplit[j, 0], preferred_element_type=F32)
            p2 = jnp.dot(lhs, gsplit[j, 1], preferred_element_type=F32)
            p3 = jnp.dot(lhs, gsplit[j, 2], preferred_element_type=F32)
            low = p1[2 * rank : 3 * rank] + p2[rank : 2 * rank] + p3[:rank]
            parts.append(p1[:rank] + (p1[rank : 2 * rank] + p2[:rank] + low))
        ybuf[step, my_chan] = jnp.concatenate(parts, axis=0)
        push(ybuf.at[step], my_chan, n_chan, along_chan, step)

    def gathered(step):
        arrived(ybuf.at[step], n_chan, step)
        return orthonormal(total(ybuf.at[step], n_chan).reshape(tiles, rank, times))

    advance(gathered(0), 1)

    member_rows = member[0:GROUP]
    halves = []
    for j in range(tiles):
        r = resp[j]
        model = lax.dot_general(r, r, NT, preferred_element_type=F32)
        halves.append(jnp.dot(member_rows, model * beam_gram, precision=HIGHEST, preferred_element_type=F32))
    half = jnp.concatenate(halves, axis=0)
    nbuf[my_chan] = lax.dot_general(half, member, NT, precision=HIGHEST, preferred_element_type=F32)
    push(nbuf, my_chan, n_chan, along_chan, SUB_ITERS)
    advance(gathered(1), 2)

    arrived(nbuf, n_chan, SUB_ITERS)
    normal = total(nbuf, n_chan)
    sub = lax.broadcasted_iota(jnp.int32, (GROUP, LANES), 0)
    lane = lax.broadcasted_iota(jnp.int32, (GROUP, LANES), 1)
    eye = jnp.where(sub == lane, F32(1.0), F32(0.0))
    inv, inv_rho = [], []
    for j in range(tiles):
        mat = normal[j * GROUP : (j + 1) * GROUP]
        trace = jnp.sum(jnp.sum(mat * eye, axis=1, keepdims=True), axis=0, keepdims=True)
        recip = F32(1.0) / (F32(RHO_SCALE) * trace / F32(CL))
        inv_rho.append(recip)
        inv.append(mat * recip + eye)
    for p in range(CL):
        for j in range(tiles):
            mat = inv[j]
            col = mat[:, p : p + 1]
            row = mat[p : p + 1, :]
            d = F32(1.0) / mat[p : p + 1, p : p + 1]
            row = jnp.where(lane[0:1] == p, d, row * d)
            mat = jnp.where(lane == p, F32(0.0), mat)
            inv[j] = jnp.where(sub == p, row, mat - col * row)
    before = []
    for j in range(tiles):
        bp = jnp.dot(resp[j], vis_tile(j), preferred_element_type=F32)
        before.append(jnp.sum(bp * tb, axis=-1, keepdims=True))
        b1, b2, b3 = split3(bp)
        bsplit[j, 0] = b1.astype(BF16)
        bsplit[j, 1] = b2.astype(BF16)
        bsplit[j, 2] = b3.astype(BF16)
    b1, b2, b3 = split3(tb)
    bsplit[tiles, 0] = b1.astype(BF16)
    bsplit[tiles, 1] = b2.astype(BF16)
    bsplit[tiles, 2] = b3.astype(BF16)

    big = []
    for j in range(tiles):
        e = eye - inv[j]
        if j:
            e = pltpu.roll(e, j * GROUP, 1)
        big.append(e)
    pad = jnp.zeros((LANES - tiles * GROUP, LANES), F32)
    e1 = jnp.concatenate(big + [pad], axis=0)

    def times_of(a, b):
        return jnp.dot(a, b, precision=HIGHEST, preferred_element_type=F32)

    def fold(m):
        out = m[0:GROUP]
        for j in range(1, tiles):
            out = out + m[j * GROUP : (j + 1) * GROUP]
        return out

    def fold_lanes(m):
        out = m
        for j in range(1, tiles):
            out = out + pltpu.roll(m, LANES - j * GROUP, 1)
        return jnp.where(lax.broadcasted_iota(jnp.int32, m.shape, 1) < GROUP, out, F32(0.0))

    e2 = times_of(e1, e1)
    e3 = times_of(e2, e1)
    e4 = times_of(e2, e2)
    e5 = times_of(e2, e3)
    e6 = times_of(e3, e3)
    powers = [fold(m) for m in (e1, e2, e3, e4, e5, e6)]
    packed = fold_lanes(powers[0])
    for p in range(1, ADMM_ITERS - 1):
        packed = packed + pltpu.roll(fold_lanes(powers[p]), p * GROUP, 1)
    mbuf[my_bl] = packed
    push(mbuf, my_bl, n_bl, along_bl, SUB_ITERS + 1)
    eye_all = jnp.where(lax.rem(lane, GROUP) == sub, F32(1.0), F32(0.0))
    eye_all = jnp.where(lane < tiles * GROUP, eye_all, F32(0.0))
    powers = [eye_all] + powers

    basis = gathered(2).astype(BF16).astype(F32).reshape(tiles * rank, times)
    lhs = bsplit[...].reshape((tiles + 1) * 3 * dpad, times)
    coef = lax.dot_general(lhs, basis.astype(BF16), NT, preferred_element_type=F32)

    def joined(i):
        at = i * 3 * dpad
        return coef[at : at + dpad] + (coef[at + dpad : at + 2 * dpad] + coef[at + 2 * dpad : at + 3 * dpad])

    beam_coef = joined(tiles)
    col_lane = lax.broadcasted_iota(jnp.int32, (dpad, tiles * rank), 1)
    wide_lane = lax.broadcasted_iota(jnp.int32, (dpad, LANES), 1)
    cols = jnp.zeros((dpad, LANES), F32)
    for j in range(tiles):
        inside = (col_lane >= j * rank) & (col_lane < (j + 1) * rank)
        product = jnp.where(inside, joined(j) * beam_coef, F32(0.0))
        col = before[j] - jnp.sum(product, axis=-1, keepdims=True)
        here = (wide_lane >= j * GROUP) & (wide_lane < (j + 1) * GROUP)
        cols = jnp.where(here, col * inv_rho[j], cols)
    rhs = jnp.dot(member_rows, cols, precision=HIGHEST, preferred_element_type=F32)
    rows = [
        jnp.sum((powers[0] - powers[m]) * rhs, axis=0, keepdims=True) for m in range(1, ADMM_ITERS + 1)
    ]
    last = jnp.sum((powers[ADMM_ITERS - 1] - powers[ADMM_ITERS]) * rhs, axis=0, keepdims=True)
    out_sub = lax.broadcasted_iota(jnp.int32, (8, LANES), 0)
    block = jnp.zeros((8, LANES), F32)
    for m in range(ADMM_ITERS):
        block = jnp.where(out_sub == m, rows[m], block)
    block = fold_lanes(block)
    vbuf[my_id] = jnp.where(out_sub == ADMM_ITERS, last, block)
    push(vbuf, my_id, n_all, everyone, SUB_ITERS + 2)

    clean_stores = []
    part_lane = lax.broadcasted_iota(jnp.int32, (1, 4 * rank), 1)
    for j in range(tiles):
        own = basis[j * rank : (j + 1) * rank]
        wide = jnp.concatenate([own, own, own, jnp.zeros_like(own)], axis=0).astype(BF16)
        v = vis_tile(j)
        proj = lax.dot_general(v, wide, NT, preferred_element_type=F32)
        a, b, c = split3(proj)
        parts = jnp.where(part_lane < rank, a, jnp.where(part_lane < 2 * rank, b, c)).astype(BF16)
        correction = jnp.dot(parts, wide, preferred_element_type=F32)
        clean_ref[:, :, j * tile : (j + 1) * tile, :] = (
            (v.astype(F32) - correction).astype(BF16).reshape(2, chan_dev, tile, times)
        )
        at = (slice(None), slice(None), pl.ds(j * tile, tile), slice(None))
        clean_stores.append(pltpu.make_async_copy(clean_ref.at[at], clean_hbm.at[at], clean_sems.at[j]))
        clean_stores[-1].start()

    arrived(mbuf, n_bl, SUB_ITERS + 1)
    moments = total(mbuf, n_bl) * F32(1.0 / tiles_all)
    history = [eye]
    for p in range(ADMM_ITERS - 1):
        m = moments if p == 0 else pltpu.roll(moments, LANES - p * GROUP, 1)
        history.append(jnp.where(lane < GROUP, m, F32(0.0)))
    gain = [history[p] - F32(2.0) * history[p + 1] for p in range(ADMM_ITERS - 1)]
    local = []
    for i in range(1, ADMM_ITERS - 1):
        k = ADMM_ITERS - 2 - i
        local.append(F32(3.0) * powers[k + 1] - powers[k] - F32(2.0) * powers[k + 2])
    local.append(F32(2.0) * (powers[0] - powers[1]))
    arrived(vbuf, n_all, SUB_ITERS + 2)
    sums = total(vbuf, n_all) * F32(1.0 / tiles_all)
    mine = vbuf[my_bl]
    for i in range(1, n_chan):
        mine = mine + vbuf[i * n_bl + my_bl]
    x = mine[ADMM_ITERS : ADMM_ITERS + 1]
    cols_z = []
    spread = jnp.zeros((GROUP, LANES), F32)
    for k in range(ADMM_ITERS):
        z = sums[k : k + 1]
        if k:
            acc = gain[k - 1] * cols_z[0]
            for i in range(1, k):
                acc = acc + gain[k - 1 - i] * cols_z[i]
            z = z + jnp.sum(acc, axis=0, keepdims=True)
        if k < ADMM_ITERS - 1:
            col = jnp.sum(eye * z, axis=1, keepdims=True)
            cols_z.append(col)
            spread = spread + local[k] * col
    x = x + jnp.sum(spread, axis=0, keepdims=True)
    factor = F32((channels * tile * times) ** 0.5)
    x = jnp.broadcast_to(x * factor, (8, LANES))
    for j in range(tiles):
        at = x if j == 0 else pltpu.roll(x, LANES - j * GROUP, 1)
        gains_ref[j : j + 1, :] = at[0:1, 0:CL]
    cons_ref[...] = (z * factor)[:, 0:CL]

    for store in clean_stores:
        store.wait()
    for step in range(SUB_ITERS):
        sent(ybuf.at[step], n_chan, step)
    sent(nbuf, n_chan, SUB_ITERS)
    sent(mbuf, n_bl, SUB_ITERS + 1)
    sent(vbuf, n_all, SUB_ITERS + 2)


def copy_kernel(clean_in, gains_in, cons_in, clean_out, gains_out, cons_out, sems):
    parts, chans = clean_in.shape[:2]
    copies = [
        pltpu.make_async_copy(clean_in.at[p, c], clean_out.at[p, c], sems.at[p * chans + c])
        for p in range(parts)
        for c in range(chans)
    ]
    copies.append(pltpu.make_async_copy(gains_in, gains_out, sems.at[parts * chans]))
    copies.append(pltpu.make_async_copy(cons_in, cons_out, sems.at[parts * chans + 1]))
    for copy in copies:
        copy.start()
    for copy in copies:
        copy.wait()


def per_device(vis, station_pair_index, station_coords, dir_lm, time_beam, dir_cluster, seed_block):
    n_chan = lax.axis_size("chan")
    n_bl = lax.axis_size("bl")
    chan_dev, base_dev, times = vis.shape[1:]
    tiles, _, rank = seed_block.shape
    tile = base_dev // tiles
    dirs = dir_lm.shape[0]
    dpad = (dirs + 15) // 16 * 16
    stations = station_coords.shape[0]
    vmem = pl.BlockSpec(memory_space=pltpu.VMEM)
    anywhere = pl.BlockSpec(memory_space=pl.ANY)
    shapes = (
        jax.ShapeDtypeStruct(vis.shape, BF16),
        jax.ShapeDtypeStruct((tiles, CL), F32),
        jax.ShapeDtypeStruct((1, CL), F32),
    )
    results = pl.pallas_call(
        functools.partial(main_kernel, n_chan, n_bl, chan_dev * n_chan),
        out_shape=shapes,
        in_specs=[anywhere] * 7,
        out_specs=(anywhere, vmem, vmem),
        scratch_shapes=[
            pltpu.VMEM(vis.shape, BF16),
            pltpu.VMEM(vis.shape, BF16),
            pltpu.VMEM((2, base_dev), jnp.int32),
            pltpu.VMEM((2, stations), F32),
            pltpu.VMEM((2, dirs), F32),
            pltpu.VMEM((dirs, times), F32),
            pltpu.VMEM((1, dirs), jnp.int32),
            pltpu.VMEM((tiles, rank, times), jnp.int32),
            pltpu.VMEM((tiles, 3, times, times), BF16),
            pltpu.VMEM((tiles, dpad, 2 * chan_dev * tile), BF16),
            pltpu.VMEM((8, LANES), F32),
            pltpu.VMEM((dpad, times), F32),
            pltpu.VMEM((8, LANES), jnp.int32),
            pltpu.VMEM((GROUP, stations), F32),
            pltpu.VMEM((GROUP, base_dev), F32),
            pltpu.VMEM((tiles + 1, 3, dpad, times), BF16),
            pltpu.VMEM((SUB_ITERS, n_chan, tiles * rank, times), F32),
            pltpu.VMEM((n_chan, tiles * GROUP, LANES), F32),
            pltpu.VMEM((n_bl, GROUP, LANES), F32),
            pltpu.VMEM((n_chan * n_bl, 8, LANES), F32),
            pltpu.SemaphoreType.DMA((SUB_ITERS + 3,)),
            pltpu.SemaphoreType.DMA((SUB_ITERS + 3,)),
            pltpu.SemaphoreType.DMA((tiles,)),
            pltpu.SemaphoreType.DMA((6,)),
            pltpu.SemaphoreType.DMA((tiles,)),
        ],
        compiler_params=pltpu.CompilerParams(
            collective_id=0, has_side_effects=True, vmem_limit_bytes=60 * 1024 * 1024
        ),
    )(
        vis,
        station_pair_index.T,
        station_coords.T,
        dir_lm.T,
        time_beam,
        dir_cluster.reshape(1, dirs),
        jnp.swapaxes(seed_block, 1, 2),
    )
    clean, gains, consensus = pl.pallas_call(
        copy_kernel,
        out_shape=shapes,
        in_specs=[anywhere] * 3,
        out_specs=(anywhere,) * 3,
        scratch_shapes=[pltpu.SemaphoreType.DMA((2 * chan_dev + 2,))],
        compiler_params=pltpu.CompilerParams(vmem_limit_bytes=60 * 1024 * 1024),
    )(*results)
    return clean, gains, consensus.reshape(CL)


def solution(mesh):
    placed = (P(None, "chan", "bl", None), P("bl", None), P(), P(), P(), P(), P("bl", None, None))
    return jax.shard_map(
        per_device,
        mesh=mesh,
        in_specs=placed,
        out_specs=(P(None, "chan", "bl", None), P("bl", None), P()),
        check_vma=False,
    )
```

```python
import functools

import jax
import jax.numpy as jnp
from jax import lax
from jax.experimental import pallas as pl
from jax.experimental.pallas import tpu as pltpu
from jax.sharding import PartitionSpec as P

CL = 12
SUB_ITERS = 3
ADMM_ITERS = 6
PHASE_SCALE = 20.0
RHO_SCALE = 0.5

HIGHEST = lax.Precision.HIGHEST
MESH = pl.DeviceIdType.MESH
F32 = jnp.float32
BF16 = jnp.bfloat16
LANES = 128
GROUP = 16
NT = (((1,), (1,)), ((), ()))
TN = (((0,), (0,)), ((), ()))


def split3(x):
    a = x.astype(BF16).astype(F32)
    rest = x - a
    b = rest.astype(BF16).astype(F32)
    return a, b, rest - b


def sincos(phase):
    k = jnp.floor(phase * F32(0.6366197723675814) + F32(0.5))
    r = phase - k * F32(1.5703125)
    r = r - k * F32(4.837512969970703125e-4)
    r = r - k * F32(7.54978995489188216e-8)
    r2 = r * r
    s = r + r * r2 * (F32(-1.6666654611e-1) + r2 * (F32(8.3321608736e-3) + r2 * F32(-1.9515295891e-4)))
    c = (F32(1.0) - F32(0.5) * r2) + r2 * r2 * (
        F32(4.166664568298827e-2) + r2 * (F32(-1.388731625493765e-3) + r2 * F32(2.443315711809948e-5))
    )
    ki = k.astype(jnp.int32)
    odd = (ki & 1) == 1
    cos = jnp.where(odd, s, c)
    sin = jnp.where(odd, c, s)
    cos = jnp.where(((ki + 1) & 2) == 2, -cos, cos)
    sin = jnp.where((ki & 2) == 2, -sin, sin)
    return cos, sin


def orthonormal(rows):
    count = rows.shape[1]
    sub = lax.broadcasted_iota(jnp.int32, (1, count, 1), 1)
    for k in range(0, count, 2):
        lead = rows[:, k : k + 1, :]
        follow = rows[:, k + 1 : k + 2, :]
        dots = jnp.sum(rows * lead, axis=-1, keepdims=True)
        others = jnp.sum(rows * follow, axis=-1, keepdims=True)
        ratio = dots / dots[:, k : k + 1, :]
        mix = ratio[:, k + 1 : k + 2, :]
        follow = follow - mix * lead
        others = others - mix * dots
        coef = jnp.where(sub > k, ratio, F32(0.0))
        coef_follow = jnp.where(sub > k + 1, others / others[:, k + 1 : k + 2, :], F32(0.0))
        rows = rows - coef * lead - coef_follow * follow
    norm = jnp.sum(rows * rows, axis=-1, keepdims=True)
    return rows / jnp.sqrt(norm)


def main_kernel(
    n_chan, n_bl, channels,
    vis_hbm, pair_hbm, coords_hbm, lm_hbm, tb_hbm, cluster_hbm, seed_hbm,
    clean_hbm, gains_ref, cons_ref,
    clean_ref, vis_ref, pair_ref, coords_ref, lm_ref, tb_ref, cluster_ref, seed_ref,
    gsplit, resp, lmp, tbp, clp, coord_rows, uv_ref, bsplit,
    ybuf, nbuf, mbuf, vbuf, send_sems, recv_sems, vis_sems, load_sems, clean_sems,
):
    chan_dev, base_dev, times = vis_ref.shape[1:]
    tiles, rank = seed_ref.shape[0], seed_ref.shape[1]
    tile = base_dev // tiles
    dirs = tb_ref.shape[0]
    dpad = tbp.shape[0]
    stations = coords_ref.shape[1]
    n_all = n_chan * n_bl
    tiles_all = tiles * n_bl
    my_chan = lax.axis_index("chan")
    my_bl = lax.axis_index("bl")
    my_id = my_chan * n_bl + my_bl

    loads = [
        pltpu.make_async_copy(src, dst, load_sems.at[i])
        for i, (src, dst) in enumerate(
            (
                (seed_hbm, seed_ref),
                (pair_hbm, pair_ref),
                (coords_hbm, coords_ref),
                (lm_hbm, lm_ref),
                (tb_hbm, tb_ref),
                (cluster_hbm, cluster_ref),
            )
        )
    ]
    vis_loads = []
    for j in range(tiles):
        at = (slice(None), slice(None), pl.ds(j * tile, tile), slice(None))
        vis_loads.append(pltpu.make_async_copy(vis_hbm.at[at], vis_ref.at[at], vis_sems.at[j]))
    loads[0].start()
    for load in vis_loads:
        load.start()
    for load in loads[1:]:
        load.start()

    def everyone(off):
        other = lax.rem(my_id + off, n_all)
        return (lax.div(other, n_bl), lax.rem(other, n_bl))

    def along_chan(off):
        return (lax.rem(my_chan + off, n_chan), my_bl)

    def along_bl(off):
        return (my_chan, lax.rem(my_bl + off, n_bl))

    barrier = pltpu.get_barrier_semaphore()

    @pl.loop(1, n_all)
    def _(off):
        pl.semaphore_signal(barrier, inc=1, device_id=everyone(off), device_id_type=MESH)

    def push(buf, me, n, peer, phase):
        @pl.loop(1, n)
        def _(off):
            pltpu.make_async_remote_copy(
                src_ref=buf.at[me],
                dst_ref=buf.at[me],
                send_sem=send_sems.at[phase],
                recv_sem=recv_sems.at[phase],
                device_id=peer(off),
                device_id_type=MESH,
            ).start()

    def arrived(buf, n, phase):
        part = buf.at[pl.ds(0, n - 1)]
        pltpu.make_async_copy(part, part, recv_sems.at[phase]).wait()

    def sent(buf, n, phase):
        part = buf.at[pl.ds(0, n - 1)]
        pltpu.make_async_copy(part, part, send_sems.at[phase]).wait()

    def total(buf, n):
        out = buf[0]
        for i in range(1, n):
            out = out + buf[i]
        return out

    def vis_tile(j):
        return vis_ref[:, :, j * tile : (j + 1) * tile, :].reshape(2 * chan_dev * tile, times)

    first = []
    loads[0].wait()
    for j in range(tiles):
        vis_loads[j].wait()
        v = vis_tile(j)
        gram = lax.dot_general(v, v, TN, preferred_element_type=F32)
        g1, g2, g3 = split3(gram)
        gsplit[j, 0] = g1.astype(BF16)
        gsplit[j, 1] = g2.astype(BF16)
        gsplit[j, 2] = g3.astype(BF16)
        seed = seed_ref[j].astype(F32)
        lhs = jnp.concatenate([seed, jnp.zeros_like(seed)], axis=0).astype(BF16)
        acc = jnp.dot(lhs, gsplit[j, 2], preferred_element_type=F32)
        acc = acc + jnp.dot(lhs, gsplit[j, 1], preferred_element_type=F32)
        acc = acc + jnp.dot(lhs, gsplit[j, 0], preferred_element_type=F32)
        first.append(acc[:rank])
    ybuf[0, my_chan] = jnp.concatenate(first, axis=0)
    pl.semaphore_wait(barrier, n_all - 1)
    push(ybuf.at[0], my_chan, n_chan, along_chan, 0)

    for load in loads[1:]:
        load.wait()
    lmp[...] = jnp.zeros_like(lmp)
    lmp[0:2, 0:dirs] = lm_ref[...]
    tbp[...] = jnp.zeros_like(tbp)
    tbp[0:dirs, :] = tb_ref[...]
    clp[...] = jnp.full_like(clp, -1)
    clp[0:1, 0:dirs] = cluster_ref[...]
    c1, c2, c3 = split3(coords_ref[...])
    coord_rows[...] = jnp.zeros_like(coord_rows)
    coord_rows[0:2, :] = c1
    coord_rows[2:4, :] = c2
    coord_rows[4:6, :] = c3
    tb = tbp[...]
    beam_gram = lax.dot_general(tb, tb, NT, precision=HIGHEST, preferred_element_type=F32)
    member = jnp.where(
        lax.broadcasted_iota(jnp.int32, (LANES, dpad), 0) == clp[0:1, 0:dpad], F32(1.0), F32(0.0)
    )
    station = lax.broadcasted_iota(jnp.int32, (stations, base_dev), 0)
    pick = jnp.where(station == pair_ref[0:1, :], F32(1.0), F32(0.0)) - jnp.where(
        station == pair_ref[1:2, :], F32(1.0), F32(0.0)
    )
    uv_ref[...] = jnp.dot(coord_rows[...].astype(BF16), pick.astype(BF16), preferred_element_type=F32)
    uv = uv_ref[0:2, :] + uv_ref[2:4, :] + uv_ref[4:6, :]
    uv_ref[0:2, :] = uv
    uv_ref[2:8, :] = jnp.zeros((6, base_dev), F32)
    geo = lax.dot_general(
        lmp[:, 0:dpad], uv_ref[0:8, :], TN, precision=HIGHEST, preferred_element_type=F32
    )
    for c in range(chan_dev):
        chan = jnp.full((1, tile), my_chan * chan_dev + c, jnp.int32).astype(F32)
        scale = F32(PHASE_SCALE) * (F32(1.0) + chan / F32(channels))
        for j in range(tiles):
            cos, sin = sincos(scale * geo[:, j * tile : (j + 1) * tile])
            resp[j, :, c * tile : (c + 1) * tile] = cos.astype(BF16)
            resp[j, :, (chan_dev + c) * tile : (chan_dev + c + 1) * tile] = sin.astype(BF16)

    def advance(block, step):
        parts = []
        for j in range(tiles):
            z1, z2, z3 = split3(block[j])
            lhs = jnp.concatenate([z1, z2, z3, jnp.zeros_like(z1)], axis=0).astype(BF16)
            p1 = jnp.dot(lhs, gsplit[j, 0], preferred_element_type=F32)
            p2 = jnp.dot(lhs, gsplit[j, 1], preferred_element_type=F32)
            p3 = jnp.dot(lhs, gsplit[j, 2], preferred_element_type=F32)
            low = p1[2 * rank : 3 * rank] + p2[rank : 2 * rank] + p3[:rank]
            parts.append(p1[:rank] + (p1[rank : 2 * rank] + p2[:rank] + low))
        ybuf[step, my_chan] = jnp.concatenate(parts, axis=0)
        push(ybuf.at[step], my_chan, n_chan, along_chan, step)

    def gathered(step):
        arrived(ybuf.at[step], n_chan, step)
        return orthonormal(total(ybuf.at[step], n_chan).reshape(tiles, rank, times))

    advance(gathered(0), 1)

    member_rows = member[0:GROUP]
    halves = []
    for j in range(tiles):
        r = resp[j]
        model = lax.dot_general(r, r, NT, preferred_element_type=F32)
        halves.append(jnp.dot(member_rows, model * beam_gram, precision=HIGHEST, preferred_element_type=F32))
    half = jnp.concatenate(halves, axis=0)
    nbuf[my_chan] = lax.dot_general(half, member, NT, precision=HIGHEST, preferred_element_type=F32)
    push(nbuf, my_chan, n_chan, along_chan, SUB_ITERS)
    advance(gathered(1), 2)

    arrived(nbuf, n_chan, SUB_ITERS)
    normal = total(nbuf, n_chan)
    sub = lax.broadcasted_iota(jnp.int32, (GROUP, LANES), 0)
    lane = lax.broadcasted_iota(jnp.int32, (GROUP, LANES), 1)
    eye = jnp.where(sub == lane, F32(1.0), F32(0.0))
    inv, inv_rho = [], []
    for j in range(tiles):
        mat = normal[j * GROUP : (j + 1) * GROUP]
        trace = jnp.sum(jnp.sum(mat * eye, axis=1, keepdims=True), axis=0, keepdims=True)
        recip = F32(1.0) / (F32(RHO_SCALE) * trace / F32(CL))
        inv_rho.append(recip)
        inv.append(mat * recip + eye)
    for p in range(CL):
        for j in range(tiles):
            mat = inv[j]
            col = mat[:, p : p + 1]
            row = mat[p : p + 1, :]
            d = F32(1.0) / mat[p : p + 1, p : p + 1]
            row = jnp.where(lane[0:1] == p, d, row * d)
            mat = jnp.where(lane == p, F32(0.0), mat)
            inv[j] = jnp.where(sub == p, row, mat - col * row)
    before = []
    for j in range(tiles):
        bp = jnp.dot(resp[j], vis_tile(j), preferred_element_type=F32)
        before.append(jnp.sum(bp * tb, axis=-1, keepdims=True))
        b1, b2, b3 = split3(bp)
        bsplit[j, 0] = b1.astype(BF16)
        bsplit[j, 1] = b2.astype(BF16)
        bsplit[j, 2] = b3.astype(BF16)
    b1, b2, b3 = split3(tb)
    bsplit[tiles, 0] = b1.astype(BF16)
    bsplit[tiles, 1] = b2.astype(BF16)
    bsplit[tiles, 2] = b3.astype(BF16)

    big = []
    for j in range(tiles):
        e = eye - inv[j]
        if j:
            e = pltpu.roll(e, j * GROUP, 1)
        big.append(e)
    pad = jnp.zeros((LANES - tiles * GROUP, LANES), F32)
    e1 = jnp.concatenate(big + [pad], axis=0)

    def times_of(a, b):
        return jnp.dot(a, b, precision=HIGHEST, preferred_element_type=F32)

    def fold(m):
        out = m[0:GROUP]
        for j in range(1, tiles):
            out = out + m[j * GROUP : (j + 1) * GROUP]
        return out

    def fold_lanes(m):
        out = m
        for j in range(1, tiles):
            out = out + pltpu.roll(m, LANES - j * GROUP, 1)
        return jnp.where(lax.broadcasted_iota(jnp.int32, m.shape, 1) < GROUP, out, F32(0.0))

    e2 = times_of(e1, e1)
    e3 = times_of(e2, e1)
    e4 = times_of(e2, e2)
    e5 = times_of(e2, e3)
    e6 = times_of(e3, e3)
    powers = [fold(m) for m in (e1, e2, e3, e4, e5, e6)]
    packed = fold_lanes(powers[0])
    for p in range(1, ADMM_ITERS - 1):
        packed = packed + pltpu.roll(fold_lanes(powers[p]), p * GROUP, 1)
    mbuf[my_bl] = packed
    push(mbuf, my_bl, n_bl, along_bl, SUB_ITERS + 1)
    eye_all = jnp.where(lax.rem(lane, GROUP) == sub, F32(1.0), F32(0.0))
    eye_all = jnp.where(lane < tiles * GROUP, eye_all, F32(0.0))
    powers = [eye_all] + powers

    basis = gathered(2).astype(BF16).astype(F32).reshape(tiles * rank, times)
    lhs = bsplit[...].reshape((tiles + 1) * 3 * dpad, times)
    coef = lax.dot_general(lhs, basis.astype(BF16), NT, preferred_element_type=F32)

    def joined(i):
        at = i * 3 * dpad
        return coef[at : at + dpad] + (coef[at + dpad : at + 2 * dpad] + coef[at + 2 * dpad : at + 3 * dpad])

    beam_coef = joined(tiles)
    col_lane = lax.broadcasted_iota(jnp.int32, (dpad, tiles * rank), 1)
    wide_lane = lax.broadcasted_iota(jnp.int32, (dpad, LANES), 1)
    cols = jnp.zeros((dpad, LANES), F32)
    for j in range(tiles):
        inside = (col_lane >= j * rank) & (col_lane < (j + 1) * rank)
        product = jnp.where(inside, joined(j) * beam_coef, F32(0.0))
        col = before[j] - jnp.sum(product, axis=-1, keepdims=True)
        here = (wide_lane >= j * GROUP) & (wide_lane < (j + 1) * GROUP)
        cols = jnp.where(here, col * inv_rho[j], cols)
    rhs = jnp.dot(member_rows, cols, precision=HIGHEST, preferred_element_type=F32)
    rows = [
        jnp.sum((powers[0] - powers[m]) * rhs, axis=0, keepdims=True) for m in range(1, ADMM_ITERS + 1)
    ]
    last = jnp.sum((powers[ADMM_ITERS - 1] - powers[ADMM_ITERS]) * rhs, axis=0, keepdims=True)
    out_sub = lax.broadcasted_iota(jnp.int32, (8, LANES), 0)
    block = jnp.zeros((8, LANES), F32)
    for m in range(ADMM_ITERS):
        block = jnp.where(out_sub == m, rows[m], block)
    block = fold_lanes(block)
    vbuf[my_id] = jnp.where(out_sub == ADMM_ITERS, last, block)
    push(vbuf, my_id, n_all, everyone, SUB_ITERS + 2)

    clean_stores = []
    part_lane = lax.broadcasted_iota(jnp.int32, (1, 4 * rank), 1)
    for j in range(tiles):
        own = basis[j * rank : (j + 1) * rank]
        wide = jnp.concatenate([own, own, own, jnp.zeros_like(own)], axis=0).astype(BF16)
        v = vis_tile(j)
        proj = lax.dot_general(v, wide, NT, preferred_element_type=F32)
        a, b, c = split3(proj)
        parts = jnp.where(part_lane < rank, a, jnp.where(part_lane < 2 * rank, b, c)).astype(BF16)
        correction = jnp.dot(parts, wide, preferred_element_type=F32)
        clean_ref[:, :, j * tile : (j + 1) * tile, :] = (
            (v.astype(F32) - correction).astype(BF16).reshape(2, chan_dev, tile, times)
        )
        at = (slice(None), slice(None), pl.ds(j * tile, tile), slice(None))
        clean_stores.append(pltpu.make_async_copy(clean_ref.at[at], clean_hbm.at[at], clean_sems.at[j]))
        clean_stores[-1].start()

    arrived(mbuf, n_bl, SUB_ITERS + 1)
    moments = total(mbuf, n_bl) * F32(1.0 / tiles_all)
    history = [eye]
    for p in range(ADMM_ITERS - 1):
        m = moments if p == 0 else pltpu.roll(moments, LANES - p * GROUP, 1)
        history.append(jnp.where(lane < GROUP, m, F32(0.0)))
    gain = [history[p] - F32(2.0) * history[p + 1] for p in range(ADMM_ITERS - 1)]
    local = []
    for i in range(1, ADMM_ITERS - 1):
        k = ADMM_ITERS - 2 - i
        local.append(F32(3.0) * powers[k + 1] - powers[k] - F32(2.0) * powers[k + 2])
    local.append(F32(2.0) * (powers[0] - powers[1]))
    arrived(vbuf, n_all, SUB_ITERS + 2)
    sums = total(vbuf, n_all) * F32(1.0 / tiles_all)
    mine = vbuf[my_bl]
    for i in range(1, n_chan):
        mine = mine + vbuf[i * n_bl + my_bl]
    x = mine[ADMM_ITERS : ADMM_ITERS + 1]
    cols_z = []
    spread = jnp.zeros((GROUP, LANES), F32)
    for k in range(ADMM_ITERS):
        z = sums[k : k + 1]
        if k:
            acc = gain[k - 1] * cols_z[0]
            for i in range(1, k):
                acc = acc + gain[k - 1 - i] * cols_z[i]
            z = z + jnp.sum(acc, axis=0, keepdims=True)
        if k < ADMM_ITERS - 1:
            col = jnp.sum(eye * z, axis=1, keepdims=True)
            cols_z.append(col)
            spread = spread + local[k] * col
    x = x + jnp.sum(spread, axis=0, keepdims=True)
    factor = F32((channels * tile * times) ** 0.5)
    x = jnp.broadcast_to(x * factor, (8, LANES))
    for j in range(tiles):
        at = x if j == 0 else pltpu.roll(x, LANES - j * GROUP, 1)
        gains_ref[j : j + 1, :] = at[0:1, 0:CL]
    cons_ref[...] = (z * factor)[:, 0:CL]

    for store in clean_stores:
        store.wait()
    for step in range(SUB_ITERS):
        sent(ybuf.at[step], n_chan, step)
    sent(nbuf, n_chan, SUB_ITERS)
    sent(mbuf, n_bl, SUB_ITERS + 1)
    sent(vbuf, n_all, SUB_ITERS + 2)


def copy_kernel(clean_in, gains_in, cons_in, clean_out, gains_out, cons_out, held, in_sems, out_sems):
    gains_out[...] = gains_in[...]
    cons_out[...] = cons_in[...]
    parts, chans = clean_in.shape[:2]
    blocks = [(p, c) for p in range(parts) for c in range(chans)]
    loads, stores = [], []
    for i, (p, c) in enumerate(blocks):
        loads.append(pltpu.make_async_copy(clean_in.at[p, c], held.at[p, c], in_sems.at[i]))
        stores.append(pltpu.make_async_copy(held.at[p, c], clean_out.at[p, c], out_sems.at[i]))
        loads[i].start()
    for i in range(len(blocks)):
        loads[i].wait()
        stores[i].start()
    for store in stores:
        store.wait()


def per_device(vis, station_pair_index, station_coords, dir_lm, time_beam, dir_cluster, seed_block):
    n_chan = lax.axis_size("chan")
    n_bl = lax.axis_size("bl")
    chan_dev, base_dev, times = vis.shape[1:]
    tiles, _, rank = seed_block.shape
    tile = base_dev // tiles
    dirs = dir_lm.shape[0]
    dpad = (dirs + 15) // 16 * 16
    stations = station_coords.shape[0]
    vmem = pl.BlockSpec(memory_space=pltpu.VMEM)
    anywhere = pl.BlockSpec(memory_space=pl.ANY)
    shapes = (
        jax.ShapeDtypeStruct(vis.shape, BF16),
        jax.ShapeDtypeStruct((tiles, CL), F32),
        jax.ShapeDtypeStruct((1, CL), F32),
    )
    results = pl.pallas_call(
        functools.partial(main_kernel, n_chan, n_bl, chan_dev * n_chan),
        out_shape=shapes,
        in_specs=[anywhere] * 7,
        out_specs=(anywhere, vmem, vmem),
        scratch_shapes=[
            pltpu.VMEM(vis.shape, BF16),
            pltpu.VMEM(vis.shape, BF16),
            pltpu.VMEM((2, base_dev), jnp.int32),
            pltpu.VMEM((2, stations), F32),
            pltpu.VMEM((2, dirs), F32),
            pltpu.VMEM((dirs, times), F32),
            pltpu.VMEM((1, dirs), jnp.int32),
            pltpu.VMEM((tiles, rank, times), jnp.int32),
            pltpu.VMEM((tiles, 3, times, times), BF16),
            pltpu.VMEM((tiles, dpad, 2 * chan_dev * tile), BF16),
            pltpu.VMEM((8, LANES), F32),
            pltpu.VMEM((dpad, times), F32),
            pltpu.VMEM((8, LANES), jnp.int32),
            pltpu.VMEM((GROUP, stations), F32),
            pltpu.VMEM((GROUP, base_dev), F32),
            pltpu.VMEM((tiles + 1, 3, dpad, times), BF16),
            pltpu.VMEM((SUB_ITERS, n_chan, tiles * rank, times), F32),
            pltpu.VMEM((n_chan, tiles * GROUP, LANES), F32),
            pltpu.VMEM((n_bl, GROUP, LANES), F32),
            pltpu.VMEM((n_chan * n_bl, 8, LANES), F32),
            pltpu.SemaphoreType.DMA((SUB_ITERS + 3,)),
            pltpu.SemaphoreType.DMA((SUB_ITERS + 3,)),
            pltpu.SemaphoreType.DMA((tiles,)),
            pltpu.SemaphoreType.DMA((6,)),
            pltpu.SemaphoreType.DMA((tiles,)),
        ],
        compiler_params=pltpu.CompilerParams(
            collective_id=0, has_side_effects=True, vmem_limit_bytes=60 * 1024 * 1024
        ),
    )(
        vis,
        station_pair_index.T,
        station_coords.T,
        dir_lm.T,
        time_beam,
        dir_cluster.reshape(1, dirs),
        jnp.swapaxes(seed_block, 1, 2),
    )
    clean, gains, consensus = pl.pallas_call(
        copy_kernel,
        out_shape=shapes,
        in_specs=[anywhere, vmem, vmem],
        out_specs=(anywhere, vmem, vmem),
        scratch_shapes=[
            pltpu.VMEM(vis.shape, BF16),
            pltpu.SemaphoreType.DMA((2 * chan_dev,)),
            pltpu.SemaphoreType.DMA((2 * chan_dev,)),
        ],
        compiler_params=pltpu.CompilerParams(vmem_limit_bytes=60 * 1024 * 1024),
    )(*results)
    return clean, gains, consensus.reshape(CL)


def solution(mesh):
    placed = (P(None, "chan", "bl", None), P("bl", None), P(), P(), P(), P(), P("bl", None, None))
    return jax.shard_map(
        per_device,
        mesh=mesh,
        in_specs=placed,
        out_specs=(P(None, "chan", "bl", None), P("bl", None), P()),
        check_vma=False,
    )
```
